32 devices in a mesh: tm: 8 (over y, x, core), space: 4 (over z).
Axes of the slice: x: 2, y: 2, z: 4, core: 2. Of those that a mesh axis runs over, the one named last changes fastest.
Arguments:
- start_field: float32 [8, 64, 1024], P('tm', None, 'space'), may hold values from -6 to 6
- play_level: int32 [8, 64, 1024], P('tm', None, 'space'), may hold values from -8 to 8
- stiffness: float32 [4, 64, 64, 1024], P(None, None, None, 'space')
- columns: int32 [4, 1024], P(None, 'space'), may hold values from 0 to 287, as said below
- play_width: float32 [64, 1024], P(None, 'space'), may hold values from 0.05 to 0.5
- coil: float32 [3, 64, 1024], P(None, None, 'space'), may hold values from -6 to 6
- newton_counts: int32 [8, 4], P('tm'), may hold values from 1 to 3, as said below
Outputs:
- field_starts: float32 [8, 64, 1024], P('tm', None, 'space')
- play_starts: float32 [8, 64, 1024], P('tm', None, 'space')
The draws below stay inside these ranges and needn't reach their ends.
Inputs may be any that keep to these rules, and one draw needn't show every extreme that they name: `columns`: slot 0 is the block itself, 16 plus its local index; every slot lies within 16 of that, counting the partition's blocks extended by 16 interface blocks on each side. `newton_counts`: the same for all partitions of a slice.
All inputs are finite; a program needn't handle non-finite values.
Results may differ from the reference program's by a relative error of at most 0.00016.
Values sent between devices are 32-bit elements; how exact they have to be, the bound alone decides.
A program may use at most 64 MiB of HBM per device.

```python
import math
import jax
import jax.numpy as jnp
from jax import lax

BLK = 64
NNZ = 4
NBLK = 256
NIF = 16
STEPS = 4
NEWT = 3
ITERS = 2
SLICES = 8
NCOL = 1024


def draw_stiffness(key, part):
    key_diag, key_off = jax.random.split(key)
    diag_vals = jax.random.uniform(key_diag, (BLK, NCOL), jnp.float32, 2.0, 4.0)
    off = 0.015 * jax.random.normal(key_off, (NNZ, BLK, BLK, NCOL), jnp.float32)
    eye_block = jnp.eye(BLK, dtype=jnp.float32)[:, :, None]
    first = off[0] * (1.0 - eye_block) + eye_block * diag_vals[None, :, :]
    return jnp.concatenate([first[None], off[1:]], axis=0)


def draw_columns(key, part):
    local = jnp.arange(NCOL, dtype=jnp.int32) % NBLK
    shifts = jax.random.randint(key, (NNZ - 1, NCOL), -NIF, NIF + 1, dtype=jnp.int32)
    first_row = jnp.where(local == 0, -NIF, jnp.where(local == NBLK - 1, NIF, shifts[0]))
    shifts = jnp.concatenate([jnp.zeros((1, NCOL), jnp.int32), first_row[None], shifts[1:]], axis=0)
    return (local[None, :] + NIF + shifts).astype(jnp.int32)


def draw_newton_counts(key, part):
    key_vals, key_top, key_low = jax.random.split(key, 3)
    total = SLICES * STEPS
    flat = jax.random.randint(key_vals, (total,), 1, NEWT + 1, dtype=jnp.int32)
    top_at = jax.random.randint(key_top, (), 0, total, dtype=jnp.int32)
    low_at = (top_at + 1 + jax.random.randint(key_low, (), 0, total - 1, dtype=jnp.int32)) % total
    spots = jnp.arange(total, dtype=jnp.int32)
    flat = jnp.where(spots == top_at, NEWT, jnp.where(spots == low_at, 1, flat))
    return flat.reshape(SLICES, STEPS)


def set_ends(result, own_key, least, top_value):
    spot = [jax.random.randint(jax.random.fold_in(own_key, axis), (), 0, length) for axis, length in enumerate(result.shape)]
    longest = result.shape.index(max(result.shape))
    beside = spot[:longest] + [(spot[longest] + 1) % result.shape[longest]] + spot[longest + 1:]
    return result.at[tuple(spot)].set(least).at[tuple(beside)].set(top_value)


def shard_levels(rng, dims, shards, smallest, high):
    gain, own = 1.0, jax.random.fold_in(rng, 6)
    for dim, blocks in shards:
        heights = jnp.exp(jax.random.uniform(jax.random.fold_in(own, dim), (blocks,), jnp.float32, smallest / len(shards), high / len(shards)))
        gain = gain * jnp.repeat(heights, dims[dim] // blocks).reshape([-1 if axis == dim else 1 for axis in range(len(dims))])
    return gain


def gaussian(own_key, shape, width, reach, cuts=(), kind=jnp.bfloat16):
    values = width * jax.random.normal(own_key, shape, jnp.float32)
    if cuts:
        values = values * shard_levels(own_key, shape, cuts, -0.22, 0.18)
    return jnp.clip(values, -reach, reach).astype(kind)


def setup_inputs(seed: int = 0) -> dict:
    seeds = jax.random.split(jax.random.key(seed), 8)
    return {
        "start_field": gaussian(seeds[0], (SLICES, BLK, NCOL), 1.0, 6.0, ((0, 8), (2, 4)), jnp.float32),
        "play_level": set_ends(jax.random.randint(seeds[1], (SLICES, BLK, NCOL), -8, 9), jax.random.fold_in(seeds[1], 1), -8, 8).astype(jnp.int32),
        "stiffness": draw_stiffness(jax.random.fold_in(seeds[7], 71), 0),
        "columns": draw_columns(jax.random.fold_in(seeds[7], 71), 0),
        "play_width": jnp.clip(jnp.exp(math.log(0.5) - 2.3025851 * jax.random.uniform(seeds[4], (BLK, NCOL), jnp.float32) ** shard_levels(seeds[4], (BLK, NCOL), ((1, 4),), -0.2, 0.2)), 0.05, 0.5),
        "coil": gaussian(seeds[5], (3, BLK, NCOL), 1.0, 6.0, ((2, 4),), jnp.float32),
        "newton_counts": draw_newton_counts(jax.random.fold_in(seeds[7], 71), 0),
    }


tau_step = 0.5
play_gain = 1.0
play_quantum = 0.05


def reference(start_field, play_level, stiffness, columns, play_width, coil, newton_counts):
    picks = jnp.arange(BLK, dtype=jnp.int32)
    diag_entries = stiffness[0][picks, picks, :]
    jacobi = 1.0 + tau_step * (diag_entries + play_gain)
    damping = 1.0 / jacobi
    offsets = (jnp.arange(NCOL, dtype=jnp.int32) // NBLK) * NBLK
    global_cols = (offsets[None, :] + columns).astype(jnp.int32)
    phases = jnp.arange(3, dtype=jnp.float32) * (2.0 * math.pi / 3.0)

    def apply_stiffness(field):
        padded = jnp.pad(field, ((0, 0), (0, 0), (NIF, NIF)))
        picked = padded[:, :, global_cols]
        return jnp.einsum("sabj,gbsj->gaj", stiffness, picked, precision=lax.Precision.HIGHEST)

    def fine(field, play_state):
        for step in range(STEPS):
            moment = (jnp.arange(SLICES, dtype=jnp.float32) * STEPS + (step + 1)) * (2.0 * math.pi / (SLICES * STEPS))
            waves = jnp.sin(moment[:, None] + phases[None, :])
            source = waves[:, 0, None, None] * coil[0] + waves[:, 1, None, None] * coil[1] + waves[:, 2, None, None] * coil[2]
            counts = newton_counts[:, step][:, None, None]
            guess = field
            for counter in range(NEWT):
                bound = jnp.minimum(jnp.maximum(play_state, guess - play_width), guess + play_width)
                resid = guess - field - tau_step * (source - apply_stiffness(guess) - play_gain * bound)
                guess = jnp.where(counter < counts, guess - resid / jacobi, guess)
            play_state = jnp.minimum(jnp.maximum(play_state, guess - play_width), guess + play_width)
            field = guess
        return field, play_state

    field = start_field
    play_state = play_level.astype(jnp.float32) * play_quantum
    for rounds in range(ITERS):
        fine_a, fine_p = fine(field, play_state)
        extra_a = fine_a - damping * field
        extra_p = fine_p - play_state
        new_a = [fine_a[SLICES - 1]]
        new_p = [fine_p[SLICES - 1]]
        for slot in range(SLICES - 1):
            new_a.append(damping * new_a[-1] + extra_a[slot])
            new_p.append(new_p[-1] + extra_p[slot])
        field = jnp.stack(new_a)
        play_state = jnp.stack(new_p)
    return field, play_state
```

```python
import functools
import math

import jax
import jax.numpy as jnp
from jax import lax
from jax.experimental import pallas as pl
from jax.experimental.pallas import tpu as pltpu
from jax.sharding import PartitionSpec as P

NIF = 16
NEWT = 3
ITERS = 2
ROWS = 8
LANES = 128
PAIR = 2
CHUNKS = 4

tau_step = 0.5
play_gain = 1.0
play_quantum = 0.05

MESH = pl.DeviceIdType.MESH


def merge_rows(sums):
    row = lax.broadcasted_iota(jnp.int32, (ROWS, LANES), 0)
    width = 1
    while len(sums) > 1:
        low = (row & width) == 0
        sums = [
            jnp.where(low, even, odd) + pltpu.roll(jnp.where(low, odd, even), width, 0)
            for even, odd in zip(sums[::2], sums[1::2])
        ]
        width *= 2
    return sums[0]


def play(state, guess, width):
    return jnp.minimum(jnp.maximum(state, guess - width), guess + width)


def kernel(
    slices, parts,
    start_hbm, level_hbm, stiff_hbm, columns_hbm, width_hbm, coil_hbm, counts_ref,
    out_a, out_p,
    start_in, level_in, columns_in, width_in, coil_in, counts_own, counts_all, small_sem,
    raw, stiff, edge_stiff, guess, field, state, begin, damp, width_ref,
    first, picked, source, waves, index, owner, edge_index,
    near_out, near_in, edge_out, edge_in, scan_out, scan_in, last_out, last_in,
    raw_sem, input_send, input_recv, near_send, near_recv, edge_send, edge_recv,
    scan_send, scan_recv, last_send, last_recv,
):
    nnz, blk, _, local = raw.shape
    groups = blk // ROWS
    octets = groups // 2
    steps = counts_ref.shape[1]
    pairs = slices // PAIR
    position = lax.axis_index("tm")
    pair, core = position // PAIR, lax.rem(position, PAIR)
    other = position + 1 - 2 * core
    part = lax.axis_index("space")
    outer = core == 1
    has_left = outer & (part > 0)
    has_right = outer & (part < parts - 1)
    sweeps = steps * NEWT

    small = [
        pltpu.make_async_copy(from_, to, small_sem.at[k])
        for k, (from_, to) in enumerate((
            (columns_hbm, columns_in), (coil_hbm, coil_in), (width_hbm, width_in),
            (start_hbm.at[0], start_in.at[core]), (level_hbm.at[0], level_in.at[core]),
        ))
    ]
    for load in small:
        load.start()
    span = blk // CHUNKS
    loads = [
        [
            pltpu.make_async_copy(
                stiff_hbm.at[s, pl.ds(q * span, span)], raw.at[s, pl.ds(q * span, span)],
                raw_sem.at[s, q],
            )
            for q in range(CHUNKS)
        ]
        for s in range(nnz)
    ]
    for group in loads:
        for load in group:
            load.start()

    edge_in[...] = jnp.zeros_like(edge_in)
    barrier = pltpu.get_barrier_semaphore()
    for offset in range(1, pairs):
        pl.semaphore_signal(
            barrier, inc=1, device_id={"tm": lax.rem(position + PAIR * offset, slices)},
            device_id_type=MESH,
        )
    pl.semaphore_signal(barrier, inc=1, device_id={"tm": other}, device_id_type=MESH)

    @pl.when(has_left)
    def _():
        pl.semaphore_signal(barrier, inc=1, device_id={"space": part - 1}, device_id_type=MESH)

    @pl.when(has_right)
    def _():
        pl.semaphore_signal(barrier, inc=1, device_id={"space": part + 1}, device_id_type=MESH)

    lane = lax.broadcasted_iota(jnp.int32, (ROWS, LANES), 1)
    row = lax.broadcasted_iota(jnp.int32, (ROWS, LANES), 0)
    low_half = lane < LANES // 2
    mine_low = jnp.where(low_half, core, 1 - core) == 1
    sixteenth = lane // NIF
    unit = jnp.where(low_half, sixteenth, LANES // NIF - 1 - sixteenth)
    at_edge = (lane < NIF) | (lane >= LANES - NIF)
    edge_lane = jnp.where(low_half, lane & (NIF - 1), LANES - NIF + (lane & (NIF - 1)))

    def take(values, where):
        return jnp.take_along_axis(values, where, axis=1, mode="promise_in_bounds")

    def rows(g):
        return pl.ds(g * ROWS if isinstance(g, int) else pl.multiple_of(g * ROWS, ROWS), ROWS)

    tiles = (pl.ds(0, LANES), pl.ds(LANES, LANES))

    def mine(ref, *where):
        return jnp.where(mine_low, ref[(*where, tiles[0])], ref[(*where, tiles[1])])

    count_rows = jnp.zeros((ROWS, LANES), jnp.float32)
    for step in range(steps):
        count = jnp.full((ROWS, LANES), counts_ref[0, step], jnp.int32).astype(jnp.float32)
        count_rows = jnp.where(row == step, count, count_rows)
    counts_own[...] = count_rows
    counts_all[core] = count_rows

    pl.semaphore_wait(
        barrier, pairs + has_left.astype(jnp.int32) + has_right.astype(jnp.int32)
    )
    inputs = [
        pltpu.make_async_remote_copy(
            src_ref=from_, dst_ref=to, send_sem=input_send.at[k], recv_sem=input_recv.at[k],
            device_id={"tm": other}, device_id_type=MESH,
        )
        for k, (from_, to) in enumerate((
            (start_hbm.at[0], start_in.at[core]), (level_hbm.at[0], level_in.at[core]),
            (counts_own, counts_all.at[core]),
        ))
    ]
    for copy in inputs:
        copy.start()

    small[0].wait()
    place = []
    for s in range(1, nnz):
        spot = jnp.broadcast_to(mine(columns_in, slice(s, s + 1)), (ROWS, LANES)) - NIF
        place.append(spot)
        index[s - 1] = spot & (LANES - 1)
        inside = (spot >= 0) & (spot < local)
        middle = ((spot >= LANES // 2) & (spot < local - LANES // 2))
        own = jnp.where(middle, 0, 1) == core
        owner[s - 1] = jnp.where(inside, jnp.where(own, 0, 1), 2)
        near = take(spot, edge_lane)
        reach = near & (NIF - 1)
        edge_index[s - 1] = reach + jnp.where(low_half, LANES - NIF - NIF * unit, NIF * unit)

    for h in range(3):
        across = (row >= steps).astype(jnp.int32)
        moment = ((pair * PAIR + across) * steps + (row - across * steps) + 1).astype(
            jnp.float32
        ) * (2.0 * math.pi / (slices * steps))
        waves[h] = jnp.sin(moment + h * (2.0 * math.pi / 3.0))

    small[1].wait()
    small[2].wait()
    for g in range(groups):
        width_ref[rows(g)] = mine(width_in, rows(g))
        coils = [mine(coil_in, h, rows(g)) for h in range(3)]
        for step in range(steps):
            for z in range(PAIR):
                at = pl.ds(z * steps + step, 1)
                source[step, z, rows(g)] = (
                    waves[0, at] * coils[0] + waves[1, at] * coils[1] + waves[2, at] * coils[2]
                )

    small[3].wait()
    small[4].wait()
    for copy in inputs:
        copy.wait()
    for z in range(PAIR):
        for g in range(groups):
            here = (z, rows(g))
            a = mine(start_in, *here)
            p = mine(level_in, *here).astype(jnp.float32) * play_quantum
            guess[here] = a
            field[here] = a
            begin[(0, *here)] = a
            state[here] = p
            begin[(1, *here)] = p

    for s in range(nnz):
        if s > 0:
            near = take(place[s - 1], edge_lane)
            crosses = jnp.where(low_half, -1 - near, near - local) >= 0
        for q in range(CHUNKS):
            loads[s][q].wait()

            @pl.loop(q * span, (q + 1) * span)
            def _(a):
                blocks = []
                for b in range(groups):
                    block = mine(raw, s, a, rows(b))
                    stiff[s, a, rows(b)] = block
                    blocks.append(block)
                if s > 0:
                    for v in range(octets):
                        packed = jnp.where(
                            (unit & 1) == 0,
                            take(blocks[2 * v], edge_lane), take(blocks[2 * v + 1], edge_lane),
                        )
                        edge_stiff[s - 1, a, v] = jnp.where(crosses, packed, 0.0)

        if s == 0:
            for g in range(groups):
                diag = jnp.zeros((ROWS, LANES), jnp.float32)
                for r in range(ROWS):
                    diag = jnp.where(row == r, stiff[0, g * ROWS + r, rows(g)], diag)
                damp[rows(g)] = 1.0 / (1.0 + tau_step * (diag + play_gain))

    def near_copy(slot):
        return pltpu.make_async_remote_copy(
            src_ref=near_out, dst_ref=near_in.at[slot],
            send_sem=near_send, recv_sem=near_recv.at[slot],
            device_id={"tm": other}, device_id_type=MESH,
        )

    def edge_copy(side, slot):
        return pltpu.make_async_remote_copy(
            src_ref=edge_out, dst_ref=edge_in.at[side, slot],
            send_sem=edge_send.at[side], recv_sem=edge_recv.at[side, slot],
            device_id={"space": part + 1 - 2 * side}, device_id_type=MESH,
        )

    def send_edges(slot):
        for v in range(octets):
            packed = guess[0, rows(2 * v)]
            for k in range(1, 2 * PAIR):
                moved = take(guess[k // 2, rows(2 * v + k % 2)], lane ^ (NIF * k))
                packed = jnp.where(unit == k, moved, packed)
            edge_out[v] = packed

        @pl.when(has_right)
        def _():
            edge_copy(0, slot).start()

        @pl.when(has_left)
        def _():
            edge_copy(1, slot).start()

    def products(slots, g):
        sums = [[None] * ROWS for _ in range(PAIR)]
        for s in slots:
            for b in range(groups):
                vectors = [
                    guess[z, rows(b)] if s == 0 else picked[z, s - 1, rows(b)]
                    for z in range(PAIR)
                ]
                for r in range(ROWS):
                    block = stiff[s, g * ROWS + r, rows(b)]
                    for z in range(PAIR):
                        term = block * vectors[z]
                        sums[z][r] = term if sums[z][r] is None else sums[z][r] + term
        return [merge_rows(sums[z]) for z in range(PAIR)]

    def active(step, counter, z):
        count = jnp.broadcast_to(counts_all[z, pl.ds(step, 1)], (ROWS, LANES))
        return jnp.full((ROWS, LANES), counter, jnp.int32).astype(jnp.float32) < count

    def sweep(before, step, counter):
        done = step * NEWT + counter
        slot = lax.rem(before + done, 2)
        more = done < sweeps - 1

        @pl.loop(0, groups)
        def _(g):
            sums = products((0,), g)
            for z in range(PAIR):
                first[z, rows(g)] = sums[z]

        near_copy(slot).wait()
        for s in range(1, nnz):
            where, whose = index[s - 1], owner[s - 1]
            for z in range(PAIR):
                for b in range(groups):
                    near = jnp.where(
                        whose == 0,
                        take(guess[z, rows(b)], where), take(near_in[slot, z, rows(b)], where),
                    )
                    picked[z, s - 1, rows(b)] = jnp.where(whose == 2, 0.0, near)

        @pl.loop(0, groups)
        def _(g):
            sums = products(range(1, nnz), g)
            for z in range(PAIR):
                first[z, rows(g)] += sums[z]

        for z in range(PAIR):
            works = active(step, counter, z)
            for g in range(groups):
                here = (z, rows(g))
                x = guess[here]
                bound = play(state[here], x, width_ref[rows(g)])
                resid = x - field[here] - tau_step * (
                    source[(step, *here)] - first[here] - play_gain * bound
                )
                x = jnp.where(works, x - resid * damp[rows(g)], x)
                guess[here] = x
                near_out[here] = x

        @pl.when(more)
        def _():
            near_copy(1 - slot).start()

        @pl.when(outer)
        def _():
            @pl.when(has_right)
            def _():
                edge_copy(0, slot).wait_send()
                edge_copy(1, slot).wait_recv()

            @pl.when(has_left)
            def _():
                edge_copy(1, slot).wait_send()
                edge_copy(0, slot).wait_recv()

            beyond = []
            for v in range(octets):
                both = jnp.where(low_half, edge_in[1, slot, v], edge_in[0, slot, v])
                beyond.append([take(both, edge_index[s]) for s in range(nnz - 1)])
            masks = [
                jnp.where(at_edge & active(step, counter, z), -tau_step, 0.0)
                for z in range(PAIR)
            ]
            for g in range(groups):
                total = merge_rows([
                    sum(
                        edge_stiff[s, g * ROWS + r, v] * beyond[v][s]
                        for s in range(nnz - 1) for v in range(octets)
                    )
                    for r in range(ROWS)
                ])
                total = total + take(total, lane ^ NIF)
                shares = (total, take(total, lane ^ (2 * NIF)))
                for z in range(PAIR):
                    here = (z, rows(g))
                    guess[here] = guess[here] + masks[z] * damp[rows(g)] * shares[z]

            @pl.when(more)
            def _():
                send_edges(1 - slot)

    own = [pl.ds(g * ROWS, ROWS) for g in range(groups)]
    for round_ in range(ITERS):
        before = round_ * sweeps
        near_out[...] = guess[...]
        near_copy(before % 2).start()

        @pl.when(outer)
        def _():
            send_edges(before % 2)

        @pl.loop(0, steps)
        def _(step):
            @pl.loop(0, NEWT)
            def _(counter):
                sweep(before, step, counter)

            for z in range(PAIR):
                for g in own:
                    x = guess[z, g]
                    state[z, g] = play(state[z, g], x, width_ref[g])
                    field[z, g] = x

        final = pair == pairs - 1
        ends = jnp.full((ROWS, LANES), pair, jnp.int32) == pairs - 1
        for g in own:
            d = damp[g]
            extra_a = [guess[z, g] - d * begin[0, z, g] for z in range(PAIR)]
            extra_p = [state[z, g] - begin[1, z, g] for z in range(PAIR)]
            scan_out[round_, 0, g] = jnp.where(ends, guess[1, g], d * extra_a[0] + extra_a[1])
            scan_out[round_, 1, g] = jnp.where(ends, state[1, g], extra_p[0] + extra_p[1])
            begin[0, 1, g] = extra_a[0]
            begin[1, 1, g] = extra_p[0]

        def scan_copy(to, slot):
            return pltpu.make_async_remote_copy(
                src_ref=scan_out.at[round_], dst_ref=scan_in.at[round_, slot],
                send_sem=scan_send.at[round_, to], recv_sem=scan_recv.at[round_, slot],
                device_id={"tm": to * PAIR + core}, device_id_type=MESH,
            )

        for to in range(pairs):
            @pl.when((pair != to) & (final | (pair < to)))
            def _():
                scan_copy(to, pair).start()

        for from_ in range(pairs):
            @pl.when((pair != from_) & ((from_ < pair) | (from_ == pairs - 1)))
            def _():
                scan_copy(from_, from_).wait_recv()

        @pl.when(final)
        def _():
            for g in own:
                scan_in[round_, pairs - 1, 0, g] = scan_out[round_, 0, g]
                scan_in[round_, pairs - 1, 1, g] = scan_out[round_, 1, g]

        for g in own:
            begin[0, 0, g] = scan_in[round_, pairs - 1, 0, g]
            begin[1, 0, g] = scan_in[round_, pairs - 1, 1, g]
        for from_ in range(pairs - 1):
            @pl.when(from_ < pair)
            def _():
                for g in own:
                    d = damp[g]
                    begin[0, 0, g] = d * d * begin[0, 0, g] + scan_in[round_, from_, 0, g]
                    begin[1, 0, g] = begin[1, 0, g] + scan_in[round_, from_, 1, g]
        for g in own:
            begin[0, 1, g] = damp[g] * begin[0, 0, g] + begin[0, 1, g]
            begin[1, 1, g] = begin[1, 0, g] + begin[1, 1, g]
            if round_ < ITERS - 1:
                for z in range(PAIR):
                    guess[z, g] = begin[0, z, g]
                    field[z, g] = begin[0, z, g]
                    state[z, g] = begin[1, z, g]
        for to in range(pairs):
            @pl.when((pair != to) & (final | (pair < to)))
            def _():
                scan_copy(to, pair).wait_send()

    for kind in range(2):
        for g in own:
            last_out[kind, g] = begin[kind, 1 - core, g]
    swap = pltpu.make_async_remote_copy(
        src_ref=last_out, dst_ref=last_in, send_sem=last_send, recv_sem=last_recv,
        device_id={"tm": other}, device_id_type=MESH,
    )
    swap.start()
    swap.wait()
    for kind, out in enumerate((out_a, out_p)):
        for g in own:
            kept, came = begin[kind, core, g], last_in[kind, g]
            out[0, g, tiles[0]] = jnp.where(mine_low, kept, came)
            out[0, g, tiles[1]] = jnp.where(mine_low, came, kept)


def on_device(start_field, play_level, stiffness, columns, play_width, coil, newton_counts):
    slices, parts = lax.axis_size("tm"), lax.axis_size("space")
    nnz, blk, _, local = stiffness.shape
    pairs = slices // PAIR
    groups, steps = blk // ROWS, newton_counts.shape[1]
    octets = groups // 2
    wave_rows = -(-PAIR * steps // ROWS) * ROWS
    vmem = pl.BlockSpec(memory_space=pltpu.VMEM)
    whole, half = (blk, local), (blk, LANES)
    f32, i32 = jnp.float32, jnp.int32
    dma = pltpu.SemaphoreType.DMA
    return pl.pallas_call(
        functools.partial(kernel, slices, parts),
        out_shape=[jax.ShapeDtypeStruct((1, *whole), f32)] * 2,
        in_specs=[
            *[pl.BlockSpec(memory_space=pltpu.HBM)] * 6,
            pl.BlockSpec(memory_space=pltpu.SMEM),
        ],
        out_specs=[vmem, vmem],
        scratch_shapes=[
            pltpu.VMEM((PAIR, *whole), f32),
            pltpu.VMEM((PAIR, *whole), i32),
            pltpu.VMEM(columns.shape, i32),
            pltpu.VMEM(whole, f32),
            pltpu.VMEM(coil.shape, f32),
            pltpu.VMEM((ROWS, LANES), f32),
            pltpu.VMEM((PAIR, ROWS, LANES), f32),
            dma((5,)),
            pltpu.VMEM(stiffness.shape, f32),
            pltpu.VMEM((nnz, blk, *half), f32),
            pltpu.VMEM((nnz - 1, blk, octets, ROWS, LANES), f32),
            pltpu.VMEM((PAIR, *half), f32),
            pltpu.VMEM((PAIR, *half), f32),
            pltpu.VMEM((PAIR, *half), f32),
            pltpu.VMEM((2, PAIR, *half), f32),
            pltpu.VMEM(half, f32),
            pltpu.VMEM(half, f32),
            pltpu.VMEM((PAIR, *half), f32),
            pltpu.VMEM((PAIR, nnz - 1, *half), f32),
            pltpu.VMEM((steps, PAIR, *half), f32),
            pltpu.VMEM((3, wave_rows, LANES), f32),
            pltpu.VMEM((nnz - 1, ROWS, LANES), i32),
            pltpu.VMEM((nnz - 1, ROWS, LANES), i32),
            pltpu.VMEM((nnz - 1, ROWS, LANES), i32),
            pltpu.VMEM((PAIR, *half), f32),
            pltpu.VMEM((2, PAIR, *half), f32),
            pltpu.VMEM((octets, ROWS, LANES), f32),
            pltpu.VMEM((2, 2, octets, ROWS, LANES), f32),
            pltpu.VMEM((ITERS, 2, *half), f32),
            pltpu.VMEM((ITERS, pairs, 2, *half), f32),
            pltpu.VMEM((2, *half), f32),
            pltpu.VMEM((2, *half), f32),
            dma((nnz, CHUNKS)),
            dma((3,)),
            dma((3,)),
            dma(()),
            dma((2,)),
            dma((2,)),
            dma((2, 2)),
            dma((ITERS, pairs)),
            dma((ITERS, pairs)),
            dma(()),
            dma(()),
        ],
        compiler_params=pltpu.CompilerParams(
            collective_id=0, has_side_effects=True, vmem_limit_bytes=63 * 1024 * 1024
        ),
        name="parareal",
    )(start_field, play_level, stiffness, columns, play_width, coil, newton_counts)


def solution(mesh):
    return jax.shard_map(
        on_device,
        mesh=mesh,
        in_specs=(
            P("tm", None, "space"),
            P("tm", None, "space"),
            P(None, None, None, "space"),
            P(None, "space"),
            P(None, "space"),
            P(None, None, "space"),
            P("tm", None),
        ),
        out_specs=(P("tm", None, "space"), P("tm", None, "space")),
        check_vma=False,
    )
```

```python
import functools
import math

import jax
import jax.numpy as jnp
from jax import lax
from jax.experimental import pallas as pl
from jax.experimental.pallas import tpu as pltpu
from jax.sharding import PartitionSpec as P

NIF = 16
NEWT = 3
ITERS = 2
ROWS = 8
LANES = 128
PAIR = 2
CHUNKS = 4

tau_step = 0.5
play_gain = 1.0
play_quantum = 0.05

MESH = pl.DeviceIdType.MESH


def merge_rows(sums):
    row = lax.broadcasted_iota(jnp.int32, (ROWS, LANES), 0)
    width = 1
    while len(sums) > 1:
        low = (row & width) == 0
        sums = [
            jnp.where(low, even, odd) + pltpu.roll(jnp.where(low, odd, even), width, 0)
            for even, odd in zip(sums[::2], sums[1::2])
        ]
        width *= 2
    return sums[0]


def play(state, guess, width):
    return jnp.minimum(jnp.maximum(state, guess - width), guess + width)


def kernel(
    slices, parts,
    start_hbm, level_hbm, stiff_hbm, columns_hbm, width_hbm, coil_hbm, counts_ref,
    out_ref,
    start_in, level_in, columns_in, width_in, coil_in, counts_own, counts_all, small_sem,
    raw, stiff, edge_stiff, guess, field, state, begin, damp, width_ref,
    first, picked, source, waves, index, owner, edge_index,
    near_out, near_in, edge_out, edge_in, edge_part, edge_damp, scan_out, scan_in, last_out, last_in,
    raw_sem, input_send, input_recv, near_send, near_recv, edge_send, edge_recv,
    scan_send, scan_recv, last_send, last_recv,
):
    nnz, blk, _, local = raw.shape
    groups = blk // ROWS
    octets = groups // 2
    steps = counts_ref.shape[1]
    pairs = slices // PAIR
    position = lax.axis_index("tm")
    pair, core = position // PAIR, lax.rem(position, PAIR)
    other = position + 1 - 2 * core
    part = lax.axis_index("space")
    outer = core == 1
    has_left = outer & (part > 0)
    has_right = outer & (part < parts - 1)
    sweeps = steps * NEWT

    small = [
        pltpu.make_async_copy(from_, to, small_sem.at[k])
        for k, (from_, to) in enumerate((
            (columns_hbm, columns_in), (coil_hbm, coil_in), (width_hbm, width_in),
            (start_hbm.at[0], start_in.at[core]), (level_hbm.at[0], level_in.at[core]),
        ))
    ]
    for load in small:
        load.start()
    span = blk // CHUNKS
    loads = [
        [
            pltpu.make_async_copy(
                stiff_hbm.at[s, pl.ds(q * span, span)], raw.at[s, pl.ds(q * span, span)],
                raw_sem.at[s, q],
            )
            for q in range(CHUNKS)
        ]
        for s in range(nnz)
    ]
    for group in loads:
        for load in group:
            load.start()

    edge_in[...] = jnp.zeros_like(edge_in)
    barrier = pltpu.get_barrier_semaphore()
    for offset in range(1, pairs):
        pl.semaphore_signal(
            barrier, inc=1, device_id={"tm": lax.rem(position + PAIR * offset, slices)},
            device_id_type=MESH,
        )
    pl.semaphore_signal(barrier, inc=1, device_id={"tm": other}, device_id_type=MESH)

    @pl.when(has_left)
    def _():
        pl.semaphore_signal(barrier, inc=1, device_id={"space": part - 1}, device_id_type=MESH)

    @pl.when(has_right)
    def _():
        pl.semaphore_signal(barrier, inc=1, device_id={"space": part + 1}, device_id_type=MESH)

    lane = lax.broadcasted_iota(jnp.int32, (ROWS, LANES), 1)
    row = lax.broadcasted_iota(jnp.int32, (ROWS, LANES), 0)
    low_half = lane < LANES // 2
    mine_low = jnp.where(low_half, core, 1 - core) == 1
    unit = ((lane + NIF) // (2 * NIF)) & (2 * PAIR - 1)
    left_side = (lane & NIF) == 0
    at_edge = (lane < NIF) | (lane >= LANES - NIF)
    edge_lane = (lane & (NIF - 1)) + jnp.where(left_side, 0, LANES - NIF)

    def take(values, where):
        return jnp.take_along_axis(values, where, axis=1, mode="promise_in_bounds")

    def rows(g):
        return pl.ds(g * ROWS if isinstance(g, int) else pl.multiple_of(g * ROWS, ROWS), ROWS)

    tiles = (pl.ds(0, LANES), pl.ds(LANES, LANES))

    def mine(ref, *where):
        return jnp.where(mine_low, ref[(*where, tiles[0])], ref[(*where, tiles[1])])

    count_rows = jnp.zeros((ROWS, LANES), jnp.float32)
    for step in range(steps):
        count = jnp.full((ROWS, LANES), counts_ref[0, step], jnp.int32).astype(jnp.float32)
        count_rows = jnp.where(row == step, count, count_rows)
    counts_own[...] = count_rows
    counts_all[core] = count_rows

    pl.semaphore_wait(
        barrier, pairs + has_left.astype(jnp.int32) + has_right.astype(jnp.int32)
    )
    inputs = [
        pltpu.make_async_remote_copy(
            src_ref=from_, dst_ref=to, send_sem=input_send.at[k], recv_sem=input_recv.at[k],
            device_id={"tm": other}, device_id_type=MESH,
        )
        for k, (from_, to) in enumerate((
            (start_hbm.at[0], start_in.at[core]), (level_hbm.at[0], level_in.at[core]),
            (counts_own, counts_all.at[core]),
        ))
    ]
    for copy in inputs:
        copy.start()

    small[0].wait()
    place = []
    for s in range(1, nnz):
        spot = jnp.broadcast_to(mine(columns_in, slice(s, s + 1)), (ROWS, LANES)) - NIF
        place.append(spot)
        index[s - 1] = spot & (LANES - 1)
        inside = (spot >= 0) & (spot < local)
        middle = ((spot >= LANES // 2) & (spot < local - LANES // 2))
        own = jnp.where(middle, 0, 1) == core
        owner[s - 1] = jnp.where(inside, jnp.where(own, 0, 1), 2)
        near = take(spot, edge_lane)
        reach = near & (NIF - 1)
        opposite = (lane - (lane & (NIF - 1)) + jnp.where(left_side, LANES - NIF, NIF)) & (LANES - 1)
        edge_index[s - 1] = reach + opposite

    for h in range(3):
        across = (row >= steps).astype(jnp.int32)
        moment = ((pair * PAIR + across) * steps + (row - across * steps) + 1).astype(
            jnp.float32
        ) * (2.0 * math.pi / (slices * steps))
        waves[h] = jnp.sin(moment + h * (2.0 * math.pi / 3.0))

    small[1].wait()
    small[2].wait()
    for g in range(groups):
        width_ref[rows(g)] = mine(width_in, rows(g))
        coils = [mine(coil_in, h, rows(g)) for h in range(3)]
        for step in range(steps):
            for z in range(PAIR):
                at = pl.ds(z * steps + step, 1)
                source[step, z, rows(g)] = (
                    waves[0, at] * coils[0] + waves[1, at] * coils[1] + waves[2, at] * coils[2]
                )

    for s in range(nnz):
        if s > 0:
            near = take(place[s - 1], edge_lane)
            crosses = jnp.where(left_side, -1 - near, near - local) >= 0
        for q in range(CHUNKS):
            loads[s][q].wait()

            @pl.loop(q * span, (q + 1) * span, unroll=8)
            def _(a):
                blocks = []
                for b in range(groups):
                    block = mine(raw, s, a, rows(b))
                    stiff[s, a, rows(b)] = block
                    blocks.append(block)
                if s > 0:
                    for v in range(octets):
                        packed = jnp.where(
                            unit == 0, blocks[2 * v],
                            pltpu.roll(blocks[2 * v + 1], 2 * NIF, 1),
                        )
                        packed = jnp.where(unit < 2, packed, pltpu.roll(packed, 4 * NIF, 1))
                        edge_stiff[s - 1, a, v] = jnp.where(crosses, packed, 0.0)

        if s == 0:
            for g in range(groups):
                diag = jnp.zeros((ROWS, LANES), jnp.float32)
                for r in range(ROWS):
                    diag = jnp.where(row == r, stiff[0, g * ROWS + r, rows(g)], diag)
                damp[rows(g)] = 1.0 / (1.0 + tau_step * (diag + play_gain))

    small[3].wait()
    small[4].wait()
    for copy in inputs:
        copy.wait()
    for z in range(PAIR):
        for g in range(groups):
            here = (z, rows(g))
            a = mine(start_in, *here)
            p = mine(level_in, *here).astype(jnp.float32) * play_quantum
            guess[here] = a
            field[here] = a
            begin[(0, *here)] = a
            state[here] = p
            begin[(1, *here)] = p

    def near_copy(slot):
        return pltpu.make_async_remote_copy(
            src_ref=near_out, dst_ref=near_in.at[slot],
            send_sem=near_send, recv_sem=near_recv.at[slot],
            device_id={"tm": other}, device_id_type=MESH,
        )

    def edge_copy(side, slot):
        return pltpu.make_async_remote_copy(
            src_ref=edge_out, dst_ref=edge_in.at[side, slot],
            send_sem=edge_send.at[side], recv_sem=edge_recv.at[side, slot],
            device_id={"space": part + 1 - 2 * side}, device_id_type=MESH,
        )

    def pack(values):
        packs = []
        for v in range(octets):
            packed = values[0][2 * v]
            for k in range(1, 2 * PAIR):
                moved = pltpu.roll(values[k // 2][2 * v + k % 2], 2 * NIF * k, 1)
                packed = jnp.where(unit == k, moved, packed)
            packs.append(packed)
        return packs

    def send_edges(slot, more):
        @pl.when(has_right & more)
        def _():
            edge_copy(0, slot).start()

        @pl.when(has_left & more)
        def _():
            edge_copy(1, slot).start()

    def products(slots, g):
        sums = [[None] * ROWS for _ in range(PAIR)]
        for s in slots:
            for b in range(groups):
                vectors = [
                    guess[z, rows(b)] if s == 0 else picked[z, s - 1, rows(b)]
                    for z in range(PAIR)
                ]
                for r in range(ROWS):
                    block = stiff[s, g * ROWS + r, rows(b)]
                    for z in range(PAIR):
                        term = block * vectors[z]
                        sums[z][r] = term if sums[z][r] is None else sums[z][r] + term
        return [merge_rows(sums[z]) for z in range(PAIR)]

    def active(step, counter, z):
        count = jnp.broadcast_to(counts_all[z, pl.ds(step, 1)], (ROWS, LANES))
        return jnp.full((ROWS, LANES), counter, jnp.int32).astype(jnp.float32) < count

    def sweep(before, step, counter):
        done = step * NEWT + counter
        slot = lax.rem(before + done, 2)
        more = done < sweeps - 1

        @pl.loop(0, groups, unroll=4)
        def _(g):
            sums = products((0,), g)
            for z in range(PAIR):
                first[z, rows(g)] = sums[z]

        near_copy(slot).wait()
        for s in range(1, nnz):
            where, whose = index[s - 1], owner[s - 1]
            for z in range(PAIR):
                for b in range(groups):
                    near = jnp.where(
                        whose == 0,
                        take(guess[z, rows(b)], where), take(near_in[slot, z, rows(b)], where),
                    )
                    picked[z, s - 1, rows(b)] = jnp.where(whose == 2, 0.0, near)

        @pl.loop(0, groups, unroll=4)
        def _(g):
            sums = products(range(1, nnz), g)
            for z in range(PAIR):
                first[z, rows(g)] += sums[z]

        for z in range(PAIR):
            works = active(step, counter, z)
            for g in range(groups):
                here = (z, rows(g))
                x = guess[here]
                bound = play(state[here], x, width_ref[rows(g)])
                resid = x - field[here] - tau_step * (
                    source[(step, *here)] - first[here] - play_gain * bound
                )
                x = jnp.where(works, x - resid * damp[rows(g)], x)
                guess[here] = x
                near_out[here] = x

        @pl.when(more)
        def _():
            near_copy(1 - slot).start()

        @pl.when(outer)
        def _():
            partial = pack([[guess[z, rows(g)] for g in range(groups)] for z in range(PAIR)])
            works = jnp.where(
                unit < PAIR,
                jnp.where(active(step, counter, 0), -tau_step, 0.0),
                jnp.where(active(step, counter, 1), -tau_step, 0.0),
            )
            for v in range(octets):
                edge_part[0, v] = partial[v]
                edge_part[1, v] = works * edge_damp[v]

            @pl.when(has_right)
            def _():
                edge_copy(0, slot).wait_send()
                edge_copy(1, slot).wait_recv()

            @pl.when(has_left)
            def _():
                edge_copy(1, slot).wait_send()
                edge_copy(0, slot).wait_recv()

            beyond = []
            for v in range(octets):
                both = jnp.where(left_side, edge_in[1, slot, v], edge_in[0, slot, v])
                beyond.append([take(both, edge_index[s]) for s in range(nnz - 1)])
            even = (unit & 1) == 0
            for v in range(octets):
                totals = [
                    merge_rows([
                        sum(
                            edge_stiff[s, g * ROWS + r, w] * beyond[w][s]
                            for s in range(nnz - 1) for w in range(octets)
                        )
                        for r in range(ROWS)
                    ])
                    for g in (2 * v, 2 * v + 1)
                ]
                cross = jnp.where(even, totals[1], totals[0])
                total = jnp.where(even, totals[0], totals[1]) + jnp.where(
                    even, pltpu.roll(cross, LANES - 2 * NIF, 1), pltpu.roll(cross, 2 * NIF, 1)
                )
                edge_out[v] = edge_part[0, v] + edge_part[1, v] * total

            send_edges(1 - slot, more)
            for v in range(octets):
                packed = edge_out[v]
                for k in range(2 * PAIR):
                    here = (k // 2, rows(2 * v + k % 2))
                    back = packed if k == 0 else pltpu.roll(packed, LANES - 2 * NIF * k, 1)
                    guess[here] = jnp.where(at_edge, back, guess[here])

    own = [pl.ds(g * ROWS, ROWS) for g in range(groups)]
    for v, packed in enumerate(pack([[damp[g] for g in own]] * PAIR)):
        edge_damp[v] = packed
    for round_ in range(ITERS):
        before = round_ * sweeps
        near_out[...] = guess[...]
        near_copy(before % 2).start()

        @pl.when(outer)
        def _():
            for v, packed in enumerate(
                pack([[guess[z, rows(g)] for g in range(groups)] for z in range(PAIR)])
            ):
                edge_out[v] = packed
            send_edges(before % 2, True)

        @pl.loop(0, steps)
        def _(step):
            @pl.loop(0, NEWT)
            def _(counter):
                sweep(before, step, counter)

            for z in range(PAIR):
                for g in own:
                    x = guess[z, g]
                    state[z, g] = play(state[z, g], x, width_ref[g])
                    field[z, g] = x

        final = pair == pairs - 1
        ends = jnp.full((ROWS, LANES), pair, jnp.int32) == pairs - 1
        for g in own:
            d = damp[g]
            extra_a = [guess[z, g] - d * begin[0, z, g] for z in range(PAIR)]
            extra_p = [state[z, g] - begin[1, z, g] for z in range(PAIR)]
            scan_out[round_, 0, g] = jnp.where(ends, guess[1, g], d * extra_a[0] + extra_a[1])
            scan_out[round_, 1, g] = jnp.where(ends, state[1, g], extra_p[0] + extra_p[1])
            begin[0, 1, g] = extra_a[0]
            begin[1, 1, g] = extra_p[0]

        def scan_copy(to, slot):
            return pltpu.make_async_remote_copy(
                src_ref=scan_out.at[round_], dst_ref=scan_in.at[round_, slot],
                send_sem=scan_send.at[round_, to], recv_sem=scan_recv.at[round_, slot],
                device_id={"tm": to * PAIR + core}, device_id_type=MESH,
            )

        for to in range(pairs):
            @pl.when((pair != to) & (final | (pair < to)))
            def _():
                scan_copy(to, pair).start()

        for from_ in range(pairs):
            @pl.when((pair != from_) & ((from_ < pair) | (from_ == pairs - 1)))
            def _():
                scan_copy(from_, from_).wait_recv()

        @pl.when(final)
        def _():
            for g in own:
                scan_in[round_, pairs - 1, 0, g] = scan_out[round_, 0, g]
                scan_in[round_, pairs - 1, 1, g] = scan_out[round_, 1, g]

        for g in own:
            begin[0, 0, g] = scan_in[round_, pairs - 1, 0, g]
            begin[1, 0, g] = scan_in[round_, pairs - 1, 1, g]
        for from_ in range(pairs - 1):
            @pl.when(from_ < pair)
            def _():
                for g in own:
                    d = damp[g]
                    begin[0, 0, g] = d * d * begin[0, 0, g] + scan_in[round_, from_, 0, g]
                    begin[1, 0, g] = begin[1, 0, g] + scan_in[round_, from_, 1, g]
        for g in own:
            begin[0, 1, g] = damp[g] * begin[0, 0, g] + begin[0, 1, g]
            begin[1, 1, g] = begin[1, 0, g] + begin[1, 1, g]
            if round_ < ITERS - 1:
                for z in range(PAIR):
                    guess[z, g] = begin[0, z, g]
                    field[z, g] = begin[0, z, g]
                    state[z, g] = begin[1, z, g]
        for to in range(pairs):
            @pl.when((pair != to) & (final | (pair < to)))
            def _():
                scan_copy(to, pair).wait_send()

    for kind in range(2):
        for g in own:
            last_out[kind, g] = begin[kind, 1 - core, g]
    swap = pltpu.make_async_remote_copy(
        src_ref=last_out, dst_ref=last_in, send_sem=last_send, recv_sem=last_recv,
        device_id={"tm": other}, device_id_type=MESH,
    )
    swap.start()
    swap.wait()
    for kind in range(2):
        for g in own:
            kept, came = begin[kind, core, g], last_in[kind, g]
            out_ref[kind, 0, g, tiles[0]] = jnp.where(mine_low, kept, came)
            out_ref[kind, 0, g, tiles[1]] = jnp.where(mine_low, came, kept)


def on_device(start_field, play_level, stiffness, columns, play_width, coil, newton_counts):
    slices, parts = lax.axis_size("tm"), lax.axis_size("space")
    nnz, blk, _, local = stiffness.shape
    pairs = slices // PAIR
    groups, steps = blk // ROWS, newton_counts.shape[1]
    octets = groups // 2
    wave_rows = -(-PAIR * steps // ROWS) * ROWS
    vmem = pl.BlockSpec(memory_space=pltpu.VMEM)
    whole, half = (blk, local), (blk, LANES)
    f32, i32 = jnp.float32, jnp.int32
    dma = pltpu.SemaphoreType.DMA
    both = pl.pallas_call(
        functools.partial(kernel, slices, parts),
        out_shape=jax.ShapeDtypeStruct((2, 1, *whole), f32),
        in_specs=[
            *[pl.BlockSpec(memory_space=pltpu.HBM)] * 6,
            pl.BlockSpec(memory_space=pltpu.SMEM),
        ],
        out_specs=vmem,
        scratch_shapes=[
            pltpu.VMEM((PAIR, *whole), f32),
            pltpu.VMEM((PAIR, *whole), i32),
            pltpu.VMEM(columns.shape, i32),
            pltpu.VMEM(whole, f32),
            pltpu.VMEM(coil.shape, f32),
            pltpu.VMEM((ROWS, LANES), f32),
            pltpu.VMEM((PAIR, ROWS, LANES), f32),
            dma((5,)),
            pltpu.VMEM(stiffness.shape, f32),
            pltpu.VMEM((nnz, blk, *half), f32),
            pltpu.VMEM((nnz - 1, blk, octets, ROWS, LANES), f32),
            pltpu.VMEM((PAIR, *half), f32),
            pltpu.VMEM((PAIR, *half), f32),
            pltpu.VMEM((PAIR, *half), f32),
            pltpu.VMEM((2, PAIR, *half), f32),
            pltpu.VMEM(half, f32),
            pltpu.VMEM(half, f32),
            pltpu.VMEM((PAIR, *half), f32),
            pltpu.VMEM((PAIR, nnz - 1, *half), f32),
            pltpu.VMEM((steps, PAIR, *half), f32),
            pltpu.VMEM((3, wave_rows, LANES), f32),
            pltpu.VMEM((nnz - 1, ROWS, LANES), i32),
            pltpu.VMEM((nnz - 1, ROWS, LANES), i32),
            pltpu.VMEM((nnz - 1, ROWS, LANES), i32),
            pltpu.VMEM((PAIR, *half), f32),
            pltpu.VMEM((2, PAIR, *half), f32),
            pltpu.VMEM((octets, ROWS, LANES), f32),
            pltpu.VMEM((2, 2, octets, ROWS, LANES), f32),
            pltpu.VMEM((2, octets, ROWS, LANES), f32),
            pltpu.VMEM((octets, ROWS, LANES), f32),
            pltpu.VMEM((ITERS, 2, *half), f32),
            pltpu.VMEM((ITERS, pairs, 2, *half), f32),
            pltpu.VMEM((2, *half), f32),
            pltpu.VMEM((2, *half), f32),
            dma((nnz, CHUNKS)),
            dma((3,)),
            dma((3,)),
            dma(()),
            dma((2,)),
            dma((2,)),
            dma((2, 2)),
            dma((ITERS, pairs)),
            dma((ITERS, pairs)),
            dma(()),
            dma(()),
        ],
        compiler_params=pltpu.CompilerParams(
            collective_id=0, has_side_effects=True, vmem_limit_bytes=63 * 1024 * 1024
        ),
        name="parareal",
    )(start_field, play_level, stiffness, columns, play_width, coil, newton_counts)
    return both[0], both[1]


def solution(mesh):
    return jax.shard_map(
        on_device,
        mesh=mesh,
        in_specs=(
            P("tm", None, "space"),
            P("tm", None, "space"),
            P(None, None, None, "space"),
            P(None, "space"),
            P(None, "space"),
            P(None, None, "space"),
            P("tm", None),
        ),
        out_specs=(P("tm", None, "space"), P("tm", None, "space")),
        check_vma=False,
    )
```

```python
import functools
import math

import jax
import jax.numpy as jnp
from jax import lax
from jax.experimental import pallas as pl
from jax.experimental.pallas import tpu as pltpu
from jax.sharding import PartitionSpec as P

NIF = 16
NEWT = 3
ITERS = 2
ROWS = 8
LANES = 128
PAIR = 2
CHUNKS = 2
QUARTERS = 4
UNROLL = 4

tau_step = 0.5
play_gain = 1.0
play_quantum = 0.05

MESH = pl.DeviceIdType.MESH


def merge_rows(sums):
    row = lax.broadcasted_iota(jnp.int32, (ROWS, LANES), 0)
    width = 1
    while len(sums) > 1:
        low = (row & width) == 0
        sums = [
            jnp.where(low, even, odd) + pltpu.roll(jnp.where(low, odd, even), width, 0)
            for even, odd in zip(sums[::2], sums[1::2])
        ]
        width *= 2
    return sums[0]


def play(state, guess, width):
    return jnp.minimum(jnp.maximum(state, guess - width), guess + width)


def kernel(
    slices, parts,
    start_hbm, level_hbm, stiff_hbm, columns_hbm, width_hbm, coil_hbm, counts_ref,
    out_ref,
    start_in, level_in, columns_in, width_in, coil_in, counts_own, counts_all, small_sem,
    raw, stiff, edge_stiff, guess, field, state, begin, damp, width_ref,
    first, picked, source, waves, index, owner, edge_index, crosses,
    near_out, near_in, edge_out, edge_in, edge_part, edge_damp, scan_out, scan_in, last_out, last_in,
    raw_sem, input_send, input_recv, near_send, near_recv, edge_send, edge_recv,
    scan_send, scan_recv, last_send, last_recv,
):
    nnz, blk = stiff.shape[:2]
    local = raw.shape[-1]
    groups = blk // ROWS
    quarter = blk // QUARTERS
    lots = quarter // ROWS
    steps = counts_ref.shape[1]
    pairs = slices // PAIR
    position = lax.axis_index("tm")
    pair, core = position // PAIR, lax.rem(position, PAIR)
    other = position + 1 - 2 * core
    part = lax.axis_index("space")
    outer = core == 1
    has_left = outer & (part > 0)
    has_right = outer & (part < parts - 1)
    sweeps = steps * NEWT

    small = [
        pltpu.make_async_copy(from_, to, small_sem.at[k])
        for k, (from_, to) in enumerate((
            (columns_hbm, columns_in), (coil_hbm, coil_in), (width_hbm, width_in),
            (start_hbm.at[0], start_in.at[core]), (level_hbm.at[0], level_in.at[core]),
        ))
    ]
    for copy in small:
        copy.start()
    span = quarter // CHUNKS
    order = [*range(1, nnz), 0]

    def load(s, q):
        piece = pl.ds(q * span if isinstance(q, int) else pl.multiple_of(q * span, span), span)
        return pltpu.make_async_copy(
            stiff_hbm.at[s, :, piece], raw.at[s, :, piece], raw_sem.at[s, q]
        )

    for s in order:
        for q in range(CHUNKS):
            load(s, q).start()

    edge_in[...] = jnp.zeros_like(edge_in)
    barrier = pltpu.get_barrier_semaphore()
    for offset in range(1, pairs):
        pl.semaphore_signal(
            barrier, inc=1, device_id={"tm": lax.rem(position + PAIR * offset, slices)},
            device_id_type=MESH,
        )
    pl.semaphore_signal(barrier, inc=1, device_id={"tm": other}, device_id_type=MESH)

    @pl.when(has_left)
    def _():
        pl.semaphore_signal(barrier, inc=1, device_id={"space": part - 1}, device_id_type=MESH)

    @pl.when(has_right)
    def _():
        pl.semaphore_signal(barrier, inc=1, device_id={"space": part + 1}, device_id_type=MESH)

    lane = lax.broadcasted_iota(jnp.int32, (ROWS, LANES), 1)
    row = lax.broadcasted_iota(jnp.int32, (ROWS, LANES), 0)
    low_half = lane < LANES // 2
    mine_low = jnp.where(low_half, core, 1 - core) == 1
    even = (lane & NIF) == 0
    inner = lane & (NIF - 1)
    quarter_of = ((lane + NIF) // (2 * NIF)) & (QUARTERS - 1)
    at_edge = (lane < NIF) | (lane >= LANES - NIF)

    def take(values, where):
        return jnp.take_along_axis(values, where, axis=1, mode="promise_in_bounds")

    def rows(g):
        return pl.ds(g * ROWS if isinstance(g, int) else pl.multiple_of(g * ROWS, ROWS), ROWS)

    tiles = (pl.ds(0, LANES), pl.ds(LANES, LANES))

    def mine(ref, *where):
        return jnp.where(mine_low, ref[(*where, tiles[0])], ref[(*where, tiles[1])])

    count_rows = jnp.zeros((ROWS, LANES), jnp.float32)
    for step in range(steps):
        count = jnp.full((ROWS, LANES), counts_ref[0, step], jnp.int32).astype(jnp.float32)
        count_rows = jnp.where(row == step, count, count_rows)
    counts_own[...] = count_rows
    counts_all[core] = count_rows

    pl.semaphore_wait(
        barrier, pairs + has_left.astype(jnp.int32) + has_right.astype(jnp.int32)
    )
    inputs = [
        pltpu.make_async_remote_copy(
            src_ref=from_, dst_ref=to, send_sem=input_send.at[k], recv_sem=input_recv.at[k],
            device_id={"tm": other}, device_id_type=MESH,
        )
        for k, (from_, to) in enumerate((
            (start_hbm.at[0], start_in.at[core]), (level_hbm.at[0], level_in.at[core]),
            (counts_own, counts_all.at[core]),
        ))
    ]
    for copy in inputs:
        copy.start()

    small[0].wait()
    for s in range(1, nnz):
        spot = jnp.broadcast_to(mine(columns_in, slice(s, s + 1)), (ROWS, LANES)) - NIF
        index[s - 1] = spot & (LANES - 1)
        inside = (spot >= 0) & (spot < local)
        middle = ((spot >= LANES // 2) & (spot < local - LANES // 2))
        own = jnp.where(middle, 0, 1) == core
        owner[s - 1] = jnp.where(inside, jnp.where(own, 0, 1), 2)
        near = take(spot, inner + jnp.where(even, 0, LANES - NIF))
        crosses[s - 1] = jnp.where(jnp.where(even, -1 - near, near - local) >= 0, 1.0, 0.0)
        opposite = (near & (NIF - 1)) + jnp.where(even, LANES - NIF, 0)
        for k in range(QUARTERS):
            edge_index[s - 1, k] = (opposite + 2 * NIF * k) & (LANES - 1)

    for h in range(3):
        late = (row >= steps).astype(jnp.int32)
        moment = ((pair * PAIR + late) * steps + (row - late * steps) + 1).astype(
            jnp.float32
        ) * (2.0 * math.pi / (slices * steps))
        waves[h] = jnp.sin(moment + h * (2.0 * math.pi / 3.0))

    small[1].wait()
    small[2].wait()
    for g in range(groups):
        width_ref[rows(g)] = mine(width_in, rows(g))
        coils = [mine(coil_in, h, rows(g)) for h in range(3)]
        for step in range(steps):
            for z in range(PAIR):
                at = pl.ds(z * steps + step, 1)
                source[step, z, rows(g)] = (
                    waves[0, at] * coils[0] + waves[1, at] * coils[1] + waves[2, at] * coils[2]
                )

    @pl.loop(0, (nnz - 1) * CHUNKS)
    def _(c):
        s, q = 1 + c // CHUNKS, lax.rem(c, CHUNKS)
        load(s, q).wait()
        reaches = crosses[s - 1] == 1.0

        @pl.loop(0, span, unroll=UNROLL)
        def _(j):
            a = q * span + j
            for b in range(groups):
                packed = None
                for k in range(QUARTERS):
                    block = mine(raw, s, k, a, rows(b))
                    stiff[s, k * quarter + a, rows(b)] = block
                    moved = block if k == 0 else pltpu.roll(block, 2 * NIF * k, 1)
                    packed = moved if k == 0 else jnp.where(quarter_of == k, moved, packed)
                edge_stiff[s - 1, a, b] = jnp.where(reaches, packed, 0.0)

    @pl.loop(0, CHUNKS)
    def _(q):
        load(0, q).wait()

        @pl.loop(0, span, unroll=UNROLL)
        def _(j):
            a = q * span + j
            for k in range(QUARTERS):
                for b in range(groups):
                    stiff[0, k * quarter + a, rows(b)] = mine(raw, 0, k, a, rows(b))

    for g in range(groups):
        diag = jnp.zeros((ROWS, LANES), jnp.float32)
        for r in range(ROWS):
            diag = jnp.where(row == r, stiff[0, g * ROWS + r, rows(g)], diag)
        damp[rows(g)] = 1.0 / (1.0 + tau_step * (diag + play_gain))

    small[3].wait()
    small[4].wait()
    for copy in inputs:
        copy.wait()
    for z in range(PAIR):
        for g in range(groups):
            here = (z, rows(g))
            a = mine(start_in, *here)
            p = mine(level_in, *here).astype(jnp.float32) * play_quantum
            guess[here] = a
            field[here] = a
            begin[(0, *here)] = a
            state[here] = p
            begin[(1, *here)] = p

    def near_copy(slot):
        return pltpu.make_async_remote_copy(
            src_ref=near_out, dst_ref=near_in.at[slot],
            send_sem=near_send, recv_sem=near_recv.at[slot],
            device_id={"tm": other}, device_id_type=MESH,
        )

    def edge_copy(side, slot, z):
        return pltpu.make_async_remote_copy(
            src_ref=edge_out.at[z], dst_ref=edge_in.at[1 - side, slot, z],
            send_sem=edge_send.at[side, z], recv_sem=edge_recv.at[1 - side, slot, z],
            device_id={"space": part + 2 * side - 1}, device_id_type=MESH,
        )

    def pack(values):
        packs = []
        for j in range(lots):
            packed = values[j]
            for k in range(1, QUARTERS):
                moved = pltpu.roll(values[k * lots + j], 2 * NIF * k, 1)
                packed = jnp.where(quarter_of == k, moved, packed)
            packs.append(packed)
        return packs

    def send_edges(slot, z, more):
        @pl.when(has_left & more)
        def _():
            edge_copy(0, slot, z).start()

        @pl.when(has_right & more)
        def _():
            edge_copy(1, slot, z).start()

    def products(slots, g):
        sums = [[None] * ROWS for _ in range(PAIR)]
        for s in slots:
            for b in range(groups):
                vectors = [
                    guess[z, rows(b)] if s == 0 else picked[z, s - 1, rows(b)]
                    for z in range(PAIR)
                ]
                for r in range(ROWS):
                    block = stiff[s, g * ROWS + r, rows(b)]
                    for z in range(PAIR):
                        term = block * vectors[z]
                        sums[z][r] = term if sums[z][r] is None else sums[z][r] + term
        return [merge_rows(sums[z]) for z in range(PAIR)]

    def active(step, counter, z):
        count = jnp.broadcast_to(counts_all[z, pl.ds(step, 1)], (ROWS, LANES))
        return jnp.full((ROWS, LANES), counter, jnp.int32).astype(jnp.float32) < count

    def sweep(before, step, counter):
        done = step * NEWT + counter
        slot = lax.rem(before + done, 2)
        more = done < sweeps - 1

        @pl.loop(0, groups, unroll=4)
        def _(g):
            sums = products((0,), g)
            for z in range(PAIR):
                first[z, rows(g)] = sums[z]
            for s in range(1, nnz):
                for z in range(PAIR):
                    here = take(guess[z, rows(g)], index[s - 1])
                    picked[z, s - 1, rows(g)] = jnp.where(owner[s - 1] == 0, here, 0.0)

        near_copy(slot).wait()
        for s in range(1, nnz):
            where, whose = index[s - 1], owner[s - 1]
            for z in range(PAIR):
                for b in range(groups):
                    near = take(near_in[slot, z, rows(b)], where)
                    here = (z, s - 1, rows(b))
                    picked[here] = jnp.where(whose == 1, near, picked[here])

        @pl.loop(0, groups, unroll=4)
        def _(g):
            sums = products(range(1, nnz), g)
            for z in range(PAIR):
                first[z, rows(g)] += sums[z]

        for z in range(PAIR):
            works = active(step, counter, z)
            for g in range(groups):
                here = (z, rows(g))
                x = guess[here]
                bound = play(state[here], x, width_ref[rows(g)])
                resid = x - field[here] - tau_step * (
                    source[(step, *here)] - first[here] - play_gain * bound
                )
                x = jnp.where(works, x - resid * damp[rows(g)], x)
                guess[here] = x
                near_out[here] = x

        @pl.when(more)
        def _():
            near_copy(1 - slot).start()

        @pl.when(outer)
        def _():
            for z in range(PAIR):
                partial = pack([guess[z, rows(g)] for g in range(groups)])
                works = jnp.where(active(step, counter, z), -tau_step, 0.0)
                for j in range(lots):
                    edge_part[0, z, j] = partial[j]
                    edge_part[1, z, j] = works * edge_damp[j]

            for z in range(PAIR):
                @pl.when(has_left)
                def _():
                    edge_copy(0, slot, z).wait_send()
                    edge_copy(1, slot, z).wait_recv()

                @pl.when(has_right)
                def _():
                    edge_copy(1, slot, z).wait_send()
                    edge_copy(0, slot, z).wait_recv()

                came = [
                    jnp.where(even, edge_in[1, slot, z, j], edge_in[0, slot, z, j])
                    for j in range(lots)
                ]
                sums = [None] * quarter
                for s in range(nnz - 1):
                    for k in range(QUARTERS):
                        vectors = [take(came[j], edge_index[s, k]) for j in range(lots)]
                        for j in range(lots):
                            for a in range(quarter):
                                term = edge_stiff[s, a, k * lots + j] * vectors[j]
                                sums[a] = term if sums[a] is None else sums[a] + term
                for j in range(lots):
                    total = merge_rows(sums[j * ROWS : (j + 1) * ROWS])
                    edge_out[z, j] = edge_part[0, z, j] + edge_part[1, z, j] * total

                send_edges(1 - slot, z, more)

            for z in range(PAIR):
                for j in range(lots):
                    packed = edge_out[z, j]
                    for k in range(QUARTERS):
                        here = (z, rows(k * lots + j))
                        back = packed if k == 0 else pltpu.roll(packed, LANES - 2 * NIF * k, 1)
                        guess[here] = jnp.where(at_edge, back, guess[here])

    own = [pl.ds(g * ROWS, ROWS) for g in range(groups)]
    for j, packed in enumerate(pack([damp[g] for g in own])):
        edge_damp[j] = packed
    for round_ in range(ITERS):
        before = round_ * sweeps
        near_out[...] = guess[...]
        near_copy(before % 2).start()

        @pl.when(outer)
        def _():
            for z in range(PAIR):
                for j, packed in enumerate(pack([guess[z, g] for g in own])):
                    edge_out[z, j] = packed
                send_edges(before % 2, z, True)

        @pl.loop(0, steps)
        def _(step):
            @pl.loop(0, NEWT)
            def _(counter):
                sweep(before, step, counter)

            for z in range(PAIR):
                for g in own:
                    x = guess[z, g]
                    state[z, g] = play(state[z, g], x, width_ref[g])
                    field[z, g] = x

        final = pair == pairs - 1
        ends = jnp.full((ROWS, LANES), pair, jnp.int32) == pairs - 1
        for g in own:
            d = damp[g]
            extra_a = [guess[z, g] - d * begin[0, z, g] for z in range(PAIR)]
            extra_p = [state[z, g] - begin[1, z, g] for z in range(PAIR)]
            scan_out[round_, 0, g] = jnp.where(ends, guess[1, g], d * extra_a[0] + extra_a[1])
            scan_out[round_, 1, g] = jnp.where(ends, state[1, g], extra_p[0] + extra_p[1])
            begin[0, 1, g] = extra_a[0]
            begin[1, 1, g] = extra_p[0]

        def scan_copy(to, slot):
            return pltpu.make_async_remote_copy(
                src_ref=scan_out.at[round_], dst_ref=scan_in.at[round_, slot],
                send_sem=scan_send.at[round_, to], recv_sem=scan_recv.at[round_, slot],
                device_id={"tm": to * PAIR + core}, device_id_type=MESH,
            )

        for to in range(pairs):
            @pl.when((pair != to) & (final | (pair < to)))
            def _():
                scan_copy(to, pair).start()

        for from_ in range(pairs):
            @pl.when((pair != from_) & ((from_ < pair) | (from_ == pairs - 1)))
            def _():
                scan_copy(from_, from_).wait_recv()

        @pl.when(final)
        def _():
            for g in own:
                scan_in[round_, pairs - 1, 0, g] = scan_out[round_, 0, g]
                scan_in[round_, pairs - 1, 1, g] = scan_out[round_, 1, g]

        for g in own:
            begin[0, 0, g] = scan_in[round_, pairs - 1, 0, g]
            begin[1, 0, g] = scan_in[round_, pairs - 1, 1, g]
        for from_ in range(pairs - 1):
            @pl.when(from_ < pair)
            def _():
                for g in own:
                    d = damp[g]
                    begin[0, 0, g] = d * d * begin[0, 0, g] + scan_in[round_, from_, 0, g]
                    begin[1, 0, g] = begin[1, 0, g] + scan_in[round_, from_, 1, g]
        for g in own:
            begin[0, 1, g] = damp[g] * begin[0, 0, g] + begin[0, 1, g]
            begin[1, 1, g] = begin[1, 0, g] + begin[1, 1, g]
            if round_ < ITERS - 1:
                for z in range(PAIR):
                    guess[z, g] = begin[0, z, g]
                    field[z, g] = begin[0, z, g]
                    state[z, g] = begin[1, z, g]
        for to in range(pairs):
            @pl.when((pair != to) & (final | (pair < to)))
            def _():
                scan_copy(to, pair).wait_send()

    for kind in range(2):
        for g in own:
            last_out[kind, g] = begin[kind, 1 - core, g]
    swap = pltpu.make_async_remote_copy(
        src_ref=last_out, dst_ref=last_in, send_sem=last_send, recv_sem=last_recv,
        device_id={"tm": other}, device_id_type=MESH,
    )
    swap.start()
    swap.wait()
    for kind in range(2):
        for g in own:
            kept, came = begin[kind, core, g], last_in[kind, g]
            out_ref[kind, 0, g, tiles[0]] = jnp.where(mine_low, kept, came)
            out_ref[kind, 0, g, tiles[1]] = jnp.where(mine_low, came, kept)


def on_device(start_field, play_level, stiffness, columns, play_width, coil, newton_counts):
    slices, parts = lax.axis_size("tm"), lax.axis_size("space")
    nnz, blk, _, local = stiffness.shape
    pairs = slices // PAIR
    groups, steps = blk // ROWS, newton_counts.shape[1]
    quarter = blk // QUARTERS
    lots = quarter // ROWS
    stiffness = stiffness.reshape(nnz, QUARTERS, quarter, blk, local)
    wave_rows = -(-PAIR * steps // ROWS) * ROWS
    vmem = pl.BlockSpec(memory_space=pltpu.VMEM)
    whole, half = (blk, local), (blk, LANES)
    f32, i32 = jnp.float32, jnp.int32
    dma = pltpu.SemaphoreType.DMA
    both = pl.pallas_call(
        functools.partial(kernel, slices, parts),
        out_shape=jax.ShapeDtypeStruct((2, 1, *whole), f32),
        in_specs=[
            *[pl.BlockSpec(memory_space=pltpu.HBM)] * 6,
            pl.BlockSpec(memory_space=pltpu.SMEM),
        ],
        out_specs=vmem,
        scratch_shapes=[
            pltpu.VMEM((PAIR, *whole), f32),
            pltpu.VMEM((PAIR, *whole), i32),
            pltpu.VMEM(columns.shape, i32),
            pltpu.VMEM(whole, f32),
            pltpu.VMEM(coil.shape, f32),
            pltpu.VMEM((ROWS, LANES), f32),
            pltpu.VMEM((PAIR, ROWS, LANES), f32),
            dma((5,)),
            pltpu.VMEM(stiffness.shape, f32),
            pltpu.VMEM((nnz, blk, *half), f32),
            pltpu.VMEM((nnz - 1, quarter, groups, ROWS, LANES), f32),
            pltpu.VMEM((PAIR, *half), f32),
            pltpu.VMEM((PAIR, *half), f32),
            pltpu.VMEM((PAIR, *half), f32),
            pltpu.VMEM((2, PAIR, *half), f32),
            pltpu.VMEM(half, f32),
            pltpu.VMEM(half, f32),
            pltpu.VMEM((PAIR, *half), f32),
            pltpu.VMEM((PAIR, nnz - 1, *half), f32),
            pltpu.VMEM((steps, PAIR, *half), f32),
            pltpu.VMEM((3, wave_rows, LANES), f32),
            pltpu.VMEM((nnz - 1, ROWS, LANES), i32),
            pltpu.VMEM((nnz - 1, ROWS, LANES), i32),
            pltpu.VMEM((nnz - 1, QUARTERS, ROWS, LANES), i32),
            pltpu.VMEM((nnz - 1, ROWS, LANES), f32),
            pltpu.VMEM((PAIR, *half), f32),
            pltpu.VMEM((2, PAIR, *half), f32),
            pltpu.VMEM((PAIR, lots, ROWS, LANES), f32),
            pltpu.VMEM((2, 2, PAIR, lots, ROWS, LANES), f32),
            pltpu.VMEM((2, PAIR, lots, ROWS, LANES), f32),
            pltpu.VMEM((lots, ROWS, LANES), f32),
            pltpu.VMEM((ITERS, 2, *half), f32),
            pltpu.VMEM((ITERS, pairs, 2, *half), f32),
            pltpu.VMEM((2, *half), f32),
            pltpu.VMEM((2, *half), f32),
            dma((nnz, CHUNKS)),
            dma((3,)),
            dma((3,)),
            dma(()),
            dma((2,)),
            dma((2, PAIR)),
            dma((2, 2, PAIR)),
            dma((ITERS, pairs)),
            dma((ITERS, pairs)),
            dma(()),
            dma(()),
        ],
        compiler_params=pltpu.CompilerParams(
            collective_id=0, has_side_effects=True, vmem_limit_bytes=63 * 1024 * 1024
        ),
        name="parareal",
    )(start_field, play_level, stiffness, columns, play_width, coil, newton_counts)
    return both[0], both[1]


def solution(mesh):
    return jax.shard_map(
        on_device,
        mesh=mesh,
        in_specs=(
            P("tm", None, "space"),
            P("tm", None, "space"),
            P(None, None, None, "space"),
            P(None, "space"),
            P(None, "space"),
            P(None, None, "space"),
            P("tm", None),
        ),
        out_specs=(P("tm", None, "space"), P("tm", None, "space")),
        check_vma=False,
    )
```

```python
import functools
import math

import jax
import jax.numpy as jnp
from jax import lax
from jax.experimental import pallas as pl
from jax.experimental.pallas import tpu as pltpu
from jax.sharding import PartitionSpec as P

NIF = 16
NEWT = 3
ITERS = 2
ROWS = 8
LANES = 128
PAIR = 2
CHUNKS = 2
QUARTERS = 4
UNROLL = 4

tau_step = 0.5
play_gain = 1.0
play_quantum = 0.05

MESH = pl.DeviceIdType.MESH


def merge_rows(sums):
    row = lax.broadcasted_iota(jnp.int32, (ROWS, LANES), 0)
    width = 1
    while len(sums) > 1:
        low = (row & width) == 0
        sums = [
            jnp.where(low, even, odd) + pltpu.roll(jnp.where(low, odd, even), width, 0)
            for even, odd in zip(sums[::2], sums[1::2])
        ]
        width *= 2
    return sums[0]


def play(state, guess, width):
    return jnp.minimum(jnp.maximum(state, guess - width), guess + width)


def kernel(
    slices, parts,
    start_hbm, level_hbm, stiff_hbm, columns_hbm, width_hbm, coil_hbm, counts_hbm,
    out_ref,
    counts_ref, start_in, level_in, columns_in, width_in, coil_in, counts_own, counts_all, small_sem,
    raw, stiff, edge_stiff, guess, field, state, begin, damp, width_ref,
    first, picked, source, waves, index, owner, edge_index, crosses,
    near_out, near_in, edge_out, edge_in, edge_damp, scan_out, scan_in, last_out, last_in,
    raw_sem, input_send, input_recv, near_send, near_recv, edge_send, edge_recv,
    scan_send, scan_recv, last_send, last_recv,
):
    nnz, blk = stiff.shape[:2]
    local = raw.shape[-1]
    groups = blk // ROWS
    quarter = blk // QUARTERS
    lots = quarter // ROWS
    steps = counts_ref.shape[1]
    pairs = slices // PAIR
    position = lax.axis_index("tm")
    pair, core = position // PAIR, lax.rem(position, PAIR)
    other = position + 1 - 2 * core
    part = lax.axis_index("space")
    outer = core == 1
    has_left = outer & (part > 0)
    has_right = outer & (part < parts - 1)
    sweeps = steps * NEWT

    small = [
        pltpu.make_async_copy(from_, to, small_sem.at[k])
        for k, (from_, to) in enumerate((
            (columns_hbm, columns_in), (coil_hbm, coil_in), (width_hbm, width_in),
            (start_hbm.at[0], start_in.at[core]), (level_hbm.at[0], level_in.at[core]),
            (counts_hbm, counts_ref),
        ))
    ]
    for copy in reversed(small):
        copy.start()
    span = quarter // CHUNKS
    order = [*range(1, nnz), 0]

    def load(s, q):
        piece = pl.ds(q * span if isinstance(q, int) else pl.multiple_of(q * span, span), span)
        return pltpu.make_async_copy(
            stiff_hbm.at[s, :, piece], raw.at[s, :, piece], raw_sem.at[s, q]
        )

    for s in order:
        for q in range(CHUNKS):
            load(s, q).start()

    edge_in[...] = jnp.zeros_like(edge_in)
    barrier = pltpu.get_barrier_semaphore()
    for offset in range(1, pairs):
        pl.semaphore_signal(
            barrier, inc=1, device_id={"tm": lax.rem(position + PAIR * offset, slices)},
            device_id_type=MESH,
        )
    pl.semaphore_signal(barrier, inc=1, device_id={"tm": other}, device_id_type=MESH)

    @pl.when(has_left)
    def _():
        pl.semaphore_signal(barrier, inc=1, device_id={"space": part - 1}, device_id_type=MESH)

    @pl.when(has_right)
    def _():
        pl.semaphore_signal(barrier, inc=1, device_id={"space": part + 1}, device_id_type=MESH)

    lane = lax.broadcasted_iota(jnp.int32, (ROWS, LANES), 1)
    row = lax.broadcasted_iota(jnp.int32, (ROWS, LANES), 0)
    low_half = lane < LANES // 2
    mine_low = jnp.where(low_half, core, 1 - core) == 1
    even = (lane & NIF) == 0
    inner = lane & (NIF - 1)
    quarter_of = ((lane + NIF) // (2 * NIF)) & (QUARTERS - 1)
    at_edge = (lane < NIF) | (lane >= LANES - NIF)

    def take(values, where):
        return jnp.take_along_axis(values, where, axis=1, mode="promise_in_bounds")

    def rows(g):
        return pl.ds(g * ROWS if isinstance(g, int) else pl.multiple_of(g * ROWS, ROWS), ROWS)

    tiles = (pl.ds(0, LANES), pl.ds(LANES, LANES))

    def mine(ref, *where):
        return jnp.where(mine_low, ref[(*where, tiles[0])], ref[(*where, tiles[1])])

    small[5].wait()
    count_rows = jnp.zeros((ROWS, LANES), jnp.float32)
    for step in range(steps):
        count = jnp.full((ROWS, LANES), counts_ref[0, step], jnp.int32).astype(jnp.float32)
        count_rows = jnp.where(row == step, count, count_rows)
    counts_own[...] = count_rows
    counts_all[core] = count_rows

    pl.semaphore_wait(
        barrier, pairs + has_left.astype(jnp.int32) + has_right.astype(jnp.int32)
    )
    inputs = [
        pltpu.make_async_remote_copy(
            src_ref=from_, dst_ref=to, send_sem=input_send.at[k], recv_sem=input_recv.at[k],
            device_id={"tm": other}, device_id_type=MESH,
        )
        for k, (from_, to) in enumerate((
            (start_hbm.at[0], start_in.at[core]), (level_hbm.at[0], level_in.at[core]),
            (counts_own, counts_all.at[core]),
        ))
    ]
    for copy in inputs:
        copy.start()

    small[0].wait()
    for s in range(1, nnz):
        spot = jnp.broadcast_to(mine(columns_in, slice(s, s + 1)), (ROWS, LANES)) - NIF
        index[s - 1] = spot & (LANES - 1)
        inside = (spot >= 0) & (spot < local)
        middle = ((spot >= LANES // 2) & (spot < local - LANES // 2))
        own = jnp.where(middle, 0, 1) == core
        owner[s - 1] = jnp.where(inside, jnp.where(own, 0, 1), 2)
        near = take(spot, inner + jnp.where(even, 0, LANES - NIF))
        crosses[s - 1] = jnp.where(jnp.where(even, -1 - near, near - local) >= 0, 1.0, 0.0)
        opposite = (near & (NIF - 1)) + jnp.where(even, LANES - NIF, 0)
        for k in range(QUARTERS):
            edge_index[s - 1, k] = (opposite + 2 * NIF * k) & (LANES - 1)

    for h in range(3):
        late = (row >= steps).astype(jnp.int32)
        moment = ((pair * PAIR + late) * steps + (row - late * steps) + 1).astype(
            jnp.float32
        ) * (2.0 * math.pi / (slices * steps))
        waves[h] = jnp.sin(moment + h * (2.0 * math.pi / 3.0))

    small[1].wait()
    small[2].wait()
    for g in range(groups):
        width_ref[rows(g)] = mine(width_in, rows(g))
        coils = [mine(coil_in, h, rows(g)) for h in range(3)]
        for step in range(steps):
            for z in range(PAIR):
                at = pl.ds(z * steps + step, 1)
                source[step, z, rows(g)] = (
                    waves[0, at] * coils[0] + waves[1, at] * coils[1] + waves[2, at] * coils[2]
                )

    @pl.loop(0, (nnz - 1) * CHUNKS)
    def _(c):
        s, q = 1 + c // CHUNKS, lax.rem(c, CHUNKS)
        load(s, q).wait()
        reaches = crosses[s - 1] == 1.0

        @pl.loop(0, span, unroll=UNROLL)
        def _(j):
            a = q * span + j
            for b in range(groups):
                packed = None
                for k in range(QUARTERS):
                    block = mine(raw, s, k, a, rows(b))
                    stiff[s, k * quarter + a, rows(b)] = block
                    moved = block if k == 0 else pltpu.roll(block, 2 * NIF * k, 1)
                    packed = moved if k == 0 else jnp.where(quarter_of == k, moved, packed)
                edge_stiff[s - 1, a, b] = jnp.where(reaches, packed, 0.0)

    @pl.loop(0, CHUNKS)
    def _(q):
        load(0, q).wait()

        @pl.loop(0, span, unroll=UNROLL)
        def _(j):
            a = q * span + j
            for k in range(QUARTERS):
                for b in range(groups):
                    stiff[0, k * quarter + a, rows(b)] = mine(raw, 0, k, a, rows(b))

    for g in range(groups):
        diag = jnp.zeros((ROWS, LANES), jnp.float32)
        for r in range(ROWS):
            diag = jnp.where(row == r, stiff[0, g * ROWS + r, rows(g)], diag)
        damp[rows(g)] = 1.0 / (1.0 + tau_step * (diag + play_gain))

    small[3].wait()
    small[4].wait()
    for copy in inputs:
        copy.wait()
    for z in range(PAIR):
        for g in range(groups):
            here = (z, rows(g))
            a = mine(start_in, *here)
            p = mine(level_in, *here).astype(jnp.float32) * play_quantum
            guess[here] = a
            field[here] = a
            begin[(0, *here)] = a
            state[here] = p
            begin[(1, *here)] = p

    def near_copy(slot):
        return pltpu.make_async_remote_copy(
            src_ref=near_out, dst_ref=near_in.at[slot],
            send_sem=near_send, recv_sem=near_recv.at[slot],
            device_id={"tm": other}, device_id_type=MESH,
        )

    def edge_copy(side, slot, z):
        return pltpu.make_async_remote_copy(
            src_ref=edge_out.at[z], dst_ref=edge_in.at[1 - side, slot, z],
            send_sem=edge_send.at[side, z], recv_sem=edge_recv.at[1 - side, slot, z],
            device_id={"space": part + 2 * side - 1}, device_id_type=MESH,
        )

    def pack(values):
        packs = []
        for j in range(lots):
            packed = values[j]
            for k in range(1, QUARTERS):
                moved = pltpu.roll(values[k * lots + j], 2 * NIF * k, 1)
                packed = jnp.where(quarter_of == k, moved, packed)
            packs.append(packed)
        return packs

    def send_edges(slot, z, more):
        @pl.when(has_left & more)
        def _():
            edge_copy(0, slot, z).start()

        @pl.when(has_right & more)
        def _():
            edge_copy(1, slot, z).start()

    def products(slots, g):
        sums = [[None] * ROWS for _ in range(PAIR)]
        for s in slots:
            for b in range(groups):
                vectors = [
                    guess[z, rows(b)] if s == 0 else picked[z, s - 1, rows(b)]
                    for z in range(PAIR)
                ]
                for r in range(ROWS):
                    block = stiff[s, g * ROWS + r, rows(b)]
                    for z in range(PAIR):
                        term = block * vectors[z]
                        sums[z][r] = term if sums[z][r] is None else sums[z][r] + term
        return [merge_rows(sums[z]) for z in range(PAIR)]

    def active(step, counter, z):
        count = jnp.broadcast_to(counts_all[z, pl.ds(step, 1)], (ROWS, LANES))
        return jnp.full((ROWS, LANES), counter, jnp.int32).astype(jnp.float32) < count

    def sweep(before, step, counter):
        done = step * NEWT + counter
        slot = lax.rem(before + done, 2)
        more = done < sweeps - 1

        @pl.loop(0, groups, unroll=8)
        def _(g):
            sums = products((0,), g)
            for z in range(PAIR):
                first[z, rows(g)] = sums[z]
            for s in range(1, nnz):
                for z in range(PAIR):
                    here = take(guess[z, rows(g)], index[s - 1])
                    picked[z, s - 1, rows(g)] = jnp.where(owner[s - 1] == 0, here, 0.0)

        near_copy(slot).wait()
        for s in range(1, nnz):
            where, whose = index[s - 1], owner[s - 1]
            for z in range(PAIR):
                for b in range(groups):
                    near = take(near_in[slot, z, rows(b)], where)
                    here = (z, s - 1, rows(b))
                    picked[here] = jnp.where(whose == 1, near, picked[here])

        @pl.loop(0, groups, unroll=8)
        def _(g):
            sums = products(range(1, nnz), g)
            for z in range(PAIR):
                first[z, rows(g)] += sums[z]

        for z in range(PAIR):
            works = active(step, counter, z)
            for g in range(groups):
                here = (z, rows(g))
                x = guess[here]
                bound = play(state[here], x, width_ref[rows(g)])
                resid = x - field[here] - tau_step * (
                    source[(step, *here)] - first[here] - play_gain * bound
                )
                x = jnp.where(works, x - resid * damp[rows(g)], x)
                guess[here] = x
                near_out[here] = x

        @pl.when(more)
        def _():
            near_copy(1 - slot).start()

        @pl.when(outer)
        def _():
            def restore(z):
                for j in range(lots):
                    packed = edge_out[z, j]
                    for k in range(QUARTERS):
                        here = (z, rows(k * lots + j))
                        back = packed if k == 0 else pltpu.roll(packed, LANES - 2 * NIF * k, 1)
                        guess[here] = jnp.where(at_edge, back, guess[here])

            for z in range(PAIR):
                @pl.when(has_left)
                def _():
                    edge_copy(0, slot, z).wait_send()
                    edge_copy(1, slot, z).wait_recv()

                @pl.when(has_right)
                def _():
                    edge_copy(1, slot, z).wait_send()
                    edge_copy(0, slot, z).wait_recv()

                came = [
                    jnp.where(even, edge_in[1, slot, z, j], edge_in[0, slot, z, j])
                    for j in range(lots)
                ]
                sums = [None] * quarter
                for s in range(nnz - 1):
                    for k in range(QUARTERS):
                        vectors = [take(came[j], edge_index[s, k]) for j in range(lots)]
                        for j in range(lots):
                            for a in range(quarter):
                                term = edge_stiff[s, a, k * lots + j] * vectors[j]
                                sums[a] = term if sums[a] is None else sums[a] + term
                partial = pack([guess[z, rows(g)] for g in range(groups)])
                works = jnp.where(active(step, counter, z), -tau_step, 0.0)
                if z > 0:
                    restore(z - 1)
                for j in range(lots):
                    total = merge_rows(sums[j * ROWS : (j + 1) * ROWS])
                    edge_out[z, j] = partial[j] + works * edge_damp[j] * total

                send_edges(1 - slot, z, more)

            restore(PAIR - 1)

    own = [pl.ds(g * ROWS, ROWS) for g in range(groups)]
    for j, packed in enumerate(pack([damp[g] for g in own])):
        edge_damp[j] = packed
    for round_ in range(ITERS):
        before = round_ * sweeps
        near_out[...] = guess[...]
        near_copy(before % 2).start()

        @pl.when(outer)
        def _():
            for z in range(PAIR):
                for j, packed in enumerate(pack([guess[z, g] for g in own])):
                    edge_out[z, j] = packed
                send_edges(before % 2, z, True)

        @pl.loop(0, steps)
        def _(step):
            @pl.loop(0, NEWT)
            def _(counter):
                sweep(before, step, counter)

            for z in range(PAIR):
                for g in own:
                    x = guess[z, g]
                    state[z, g] = play(state[z, g], x, width_ref[g])
                    field[z, g] = x

        final = pair == pairs - 1
        ends = jnp.full((ROWS, LANES), pair, jnp.int32) == pairs - 1
        for g in own:
            d = damp[g]
            extra_a = [guess[z, g] - d * begin[0, z, g] for z in range(PAIR)]
            extra_p = [state[z, g] - begin[1, z, g] for z in range(PAIR)]
            scan_out[round_, 0, g] = jnp.where(ends, guess[1, g], d * extra_a[0] + extra_a[1])
            scan_out[round_, 1, g] = jnp.where(ends, state[1, g], extra_p[0] + extra_p[1])
            begin[0, 1, g] = extra_a[0]
            begin[1, 1, g] = extra_p[0]

        def scan_copy(to, slot):
            return pltpu.make_async_remote_copy(
                src_ref=scan_out.at[round_], dst_ref=scan_in.at[round_, slot],
                send_sem=scan_send.at[round_, to], recv_sem=scan_recv.at[round_, slot],
                device_id={"tm": to * PAIR + core}, device_id_type=MESH,
            )

        for to in range(pairs):
            @pl.when((pair != to) & (final | (pair < to)))
            def _():
                scan_copy(to, pair).start()

        for from_ in range(pairs):
            @pl.when((pair != from_) & ((from_ < pair) | (from_ == pairs - 1)))
            def _():
                scan_copy(from_, from_).wait_recv()

        @pl.when(final)
        def _():
            for g in own:
                scan_in[round_, pairs - 1, 0, g] = scan_out[round_, 0, g]
                scan_in[round_, pairs - 1, 1, g] = scan_out[round_, 1, g]

        for g in own:
            begin[0, 0, g] = scan_in[round_, pairs - 1, 0, g]
            begin[1, 0, g] = scan_in[round_, pairs - 1, 1, g]
        for from_ in range(pairs - 1):
            @pl.when(from_ < pair)
            def _():
                for g in own:
                    d = damp[g]
                    begin[0, 0, g] = d * d * begin[0, 0, g] + scan_in[round_, from_, 0, g]
                    begin[1, 0, g] = begin[1, 0, g] + scan_in[round_, from_, 1, g]
        for g in own:
            begin[0, 1, g] = damp[g] * begin[0, 0, g] + begin[0, 1, g]
            begin[1, 1, g] = begin[1, 0, g] + begin[1, 1, g]
            if round_ < ITERS - 1:
                for z in range(PAIR):
                    guess[z, g] = begin[0, z, g]
                    field[z, g] = begin[0, z, g]
                    state[z, g] = begin[1, z, g]
        for to in range(pairs):
            @pl.when((pair != to) & (final | (pair < to)))
            def _():
                scan_copy(to, pair).wait_send()

    for kind in range(2):
        for g in own:
            last_out[kind, g] = begin[kind, 1 - core, g]
    swap = pltpu.make_async_remote_copy(
        src_ref=last_out, dst_ref=last_in, send_sem=last_send, recv_sem=last_recv,
        device_id={"tm": other}, device_id_type=MESH,
    )
    swap.start()
    swap.wait()
    for kind in range(2):
        for g in own:
            kept, came = begin[kind, core, g], last_in[kind, g]
            out_ref[kind, 0, g, tiles[0]] = jnp.where(mine_low, kept, came)
            out_ref[kind, 0, g, tiles[1]] = jnp.where(mine_low, came, kept)


def on_device(start_field, play_level, stiffness, columns, play_width, coil, newton_counts):
    slices, parts = lax.axis_size("tm"), lax.axis_size("space")
    nnz, blk, _, local = stiffness.shape
    pairs = slices // PAIR
    groups, steps = blk // ROWS, newton_counts.shape[1]
    quarter = blk // QUARTERS
    lots = quarter // ROWS
    stiffness = stiffness.reshape(nnz, QUARTERS, quarter, blk, local)
    wave_rows = -(-PAIR * steps // ROWS) * ROWS
    vmem = pl.BlockSpec(memory_space=pltpu.VMEM)
    whole, half = (blk, local), (blk, LANES)
    f32, i32 = jnp.float32, jnp.int32
    dma = pltpu.SemaphoreType.DMA
    both = pl.pallas_call(
        functools.partial(kernel, slices, parts),
        out_shape=jax.ShapeDtypeStruct((2, 1, *whole), f32),
        in_specs=[pl.BlockSpec(memory_space=pltpu.HBM)] * 7,
        out_specs=vmem,
        scratch_shapes=[
            pltpu.SMEM(newton_counts.shape, i32),
            pltpu.VMEM((PAIR, *whole), f32),
            pltpu.VMEM((PAIR, *whole), i32),
            pltpu.VMEM(columns.shape, i32),
            pltpu.VMEM(whole, f32),
            pltpu.VMEM(coil.shape, f32),
            pltpu.VMEM((ROWS, LANES), f32),
            pltpu.VMEM((PAIR, ROWS, LANES), f32),
            dma((6,)),
            pltpu.VMEM(stiffness.shape, f32),
            pltpu.VMEM((nnz, blk, *half), f32),
            pltpu.VMEM((nnz - 1, quarter, groups, ROWS, LANES), f32),
            pltpu.VMEM((PAIR, *half), f32),
            pltpu.VMEM((PAIR, *half), f32),
            pltpu.VMEM((PAIR, *half), f32),
            pltpu.VMEM((2, PAIR, *half), f32),
            pltpu.VMEM(half, f32),
            pltpu.VMEM(half, f32),
            pltpu.VMEM((PAIR, *half), f32),
            pltpu.VMEM((PAIR, nnz - 1, *half), f32),
            pltpu.VMEM((steps, PAIR, *half), f32),
            pltpu.VMEM((3, wave_rows, LANES), f32),
            pltpu.VMEM((nnz - 1, ROWS, LANES), i32),
            pltpu.VMEM((nnz - 1, ROWS, LANES), i32),
            pltpu.VMEM((nnz - 1, QUARTERS, ROWS, LANES), i32),
            pltpu.VMEM((nnz - 1, ROWS, LANES), f32),
            pltpu.VMEM((PAIR, *half), f32),
            pltpu.VMEM((2, PAIR, *half), f32),
            pltpu.VMEM((PAIR, lots, ROWS, LANES), f32),
            pltpu.VMEM((2, 2, PAIR, lots, ROWS, LANES), f32),
            pltpu.VMEM((lots, ROWS, LANES), f32),
            pltpu.VMEM((ITERS, 2, *half), f32),
            pltpu.VMEM((ITERS, pairs, 2, *half), f32),
            pltpu.VMEM((2, *half), f32),
            pltpu.VMEM((2, *half), f32),
            dma((nnz, CHUNKS)),
            dma((3,)),
            dma((3,)),
            dma(()),
            dma((2,)),
            dma((2, PAIR)),
            dma((2, 2, PAIR)),
            dma((ITERS, pairs)),
            dma((ITERS, pairs)),
            dma(()),
            dma(()),
        ],
        compiler_params=pltpu.CompilerParams(
            collective_id=0, has_side_effects=True, vmem_limit_bytes=40 * 1024 * 1024
        ),
        name="parareal",
    )(*[
        pltpu.with_memory_space_constraint(array, pltpu.HBM)
        for array in (
            start_field, play_level, stiffness, columns, play_width, coil, newton_counts
        )
    ])
    return both[0], both[1]


def solution(mesh):
    return jax.shard_map(
        on_device,
        mesh=mesh,
        in_specs=(
            P("tm", None, "space"),
            P("tm", None, "space"),
            P(None, None, None, "space"),
            P(None, "space"),
            P(None, "space"),
            P(None, None, "space"),
            P("tm", None),
        ),
        out_specs=(P("tm", None, "space"), P("tm", None, "space")),
        check_vma=False,
    )
```

```python
import functools
import math

import jax
import jax.numpy as jnp
from jax import lax
from jax.experimental import pallas as pl
from jax.experimental.pallas import tpu as pltpu
from jax.sharding import PartitionSpec as P

NIF = 16
NEWT = 3
ITERS = 2
ROWS = 8
LANES = 128
PAIR = 2
CHUNKS = 2
QUARTERS = 4
UNROLL = 8

tau_step = 0.5
play_gain = 1.0
play_quantum = 0.05

MESH = pl.DeviceIdType.MESH


def merge_rows(sums):
    row = lax.broadcasted_iota(jnp.int32, (ROWS, LANES), 0)
    width = 1
    while len(sums) > 1:
        low = (row & width) == 0
        sums = [
            jnp.where(low, even, odd) + pltpu.roll(jnp.where(low, odd, even), width, 0)
            for even, odd in zip(sums[::2], sums[1::2])
        ]
        width *= 2
    return sums[0]


def play(state, guess, width):
    return jnp.minimum(jnp.maximum(state, guess - width), guess + width)


def kernel(
    slices, parts,
    start_hbm, level_hbm, stiff_hbm, columns_hbm, width_hbm, coil_hbm, counts_hbm,
    out_ref,
    counts_ref, start_in, level_in, columns_in, width_in, coil_in, counts_own, counts_all, small_sem,
    raw, stiff, edge_stiff, guess, field, state, begin, damp, width_ref,
    first, picked, source, waves, index, owner, edge_index, crosses,
    near_out, near_in, edge_out, edge_in, edge_damp, scan_out, scan_in, last_out, last_in,
    raw_sem, input_send, input_recv, near_send, near_recv, edge_send, edge_recv,
    scan_send, scan_recv, last_send, last_recv,
):
    nnz, blk = stiff.shape[:2]
    local = raw.shape[-1]
    groups = blk // ROWS
    quarter = blk // QUARTERS
    lots = quarter // ROWS
    steps = counts_ref.shape[1]
    pairs = slices // PAIR
    position = lax.axis_index("tm")
    pair, core = position // PAIR, lax.rem(position, PAIR)
    other = position + 1 - 2 * core
    part = lax.axis_index("space")
    outer = core == 1
    has_left = outer & (part > 0)
    has_right = outer & (part < parts - 1)
    sweeps = steps * NEWT

    small = [
        pltpu.make_async_copy(from_, to, small_sem.at[k])
        for k, (from_, to) in enumerate((
            (columns_hbm, columns_in), (coil_hbm, coil_in), (width_hbm, width_in),
            (start_hbm.at[0], start_in.at[core]), (level_hbm.at[0], level_in.at[core]),
            (counts_hbm, counts_ref),
        ))
    ]
    for copy in reversed(small):
        copy.start()
    span = quarter // CHUNKS
    order = [*range(1, nnz), 0]

    def load(s, q):
        piece = pl.ds(q * span if isinstance(q, int) else pl.multiple_of(q * span, span), span)
        return pltpu.make_async_copy(
            stiff_hbm.at[s, :, piece], raw.at[s, :, piece], raw_sem.at[s, q]
        )

    for s in order:
        for q in range(CHUNKS):
            load(s, q).start()

    edge_in[...] = jnp.zeros_like(edge_in)
    barrier = pltpu.get_barrier_semaphore()
    for offset in range(1, pairs):
        pl.semaphore_signal(
            barrier, inc=1, device_id={"tm": lax.rem(position + PAIR * offset, slices)},
            device_id_type=MESH,
        )
    pl.semaphore_signal(barrier, inc=1, device_id={"tm": other}, device_id_type=MESH)

    @pl.when(has_left)
    def _():
        pl.semaphore_signal(barrier, inc=1, device_id={"space": part - 1}, device_id_type=MESH)

    @pl.when(has_right)
    def _():
        pl.semaphore_signal(barrier, inc=1, device_id={"space": part + 1}, device_id_type=MESH)

    lane = lax.broadcasted_iota(jnp.int32, (ROWS, LANES), 1)
    row = lax.broadcasted_iota(jnp.int32, (ROWS, LANES), 0)
    low_half = lane < LANES // 2
    mine_low = jnp.where(low_half, core, 1 - core) == 1
    even = (lane & NIF) == 0
    inner = lane & (NIF - 1)
    quarter_of = ((lane + NIF) // (2 * NIF)) & (QUARTERS - 1)
    at_edge = (lane < NIF) | (lane >= LANES - NIF)

    def take(values, where):
        return jnp.take_along_axis(values, where, axis=1, mode="promise_in_bounds")

    def rows(g):
        return pl.ds(g * ROWS if isinstance(g, int) else pl.multiple_of(g * ROWS, ROWS), ROWS)

    tiles = (pl.ds(0, LANES), pl.ds(LANES, LANES))

    def mine(ref, *where):
        return jnp.where(mine_low, ref[(*where, tiles[0])], ref[(*where, tiles[1])])

    small[5].wait()
    count_rows = jnp.zeros((ROWS, LANES), jnp.float32)
    for step in range(steps):
        count = jnp.full((ROWS, LANES), counts_ref[0, step], jnp.int32).astype(jnp.float32)
        count_rows = jnp.where(row == step, count, count_rows)
    counts_own[...] = count_rows
    counts_all[core] = count_rows

    pl.semaphore_wait(
        barrier, pairs + has_left.astype(jnp.int32) + has_right.astype(jnp.int32)
    )
    inputs = [
        pltpu.make_async_remote_copy(
            src_ref=from_, dst_ref=to, send_sem=input_send.at[k], recv_sem=input_recv.at[k],
            device_id={"tm": other}, device_id_type=MESH,
        )
        for k, (from_, to) in enumerate((
            (start_hbm.at[0], start_in.at[core]), (level_hbm.at[0], level_in.at[core]),
            (counts_own, counts_all.at[core]),
        ))
    ]
    for copy in inputs:
        copy.start()

    small[0].wait()
    for s in range(1, nnz):
        spot = jnp.broadcast_to(mine(columns_in, slice(s, s + 1)), (ROWS, LANES)) - NIF
        index[s - 1] = spot & (LANES - 1)
        inside = (spot >= 0) & (spot < local)
        middle = ((spot >= LANES // 2) & (spot < local - LANES // 2))
        own = jnp.where(middle, 0, 1) == core
        owner[s - 1] = jnp.where(inside, jnp.where(own, 0, 1), 2)
        near = take(spot, inner + jnp.where(even, 0, LANES - NIF))
        crosses[s - 1] = jnp.where(jnp.where(even, -1 - near, near - local) >= 0, 1.0, 0.0)
        opposite = (near & (NIF - 1)) + jnp.where(even, LANES - NIF, 0)
        for k in range(QUARTERS):
            edge_index[s - 1, k] = (opposite + 2 * NIF * k) & (LANES - 1)

    for h in range(3):
        late = (row >= steps).astype(jnp.int32)
        moment = ((pair * PAIR + late) * steps + (row - late * steps) + 1).astype(
            jnp.float32
        ) * (2.0 * math.pi / (slices * steps))
        waves[h] = jnp.sin(moment + h * (2.0 * math.pi / 3.0))

    small[1].wait()
    small[2].wait()
    for g in range(groups):
        width_ref[rows(g)] = mine(width_in, rows(g))
        coils = [mine(coil_in, h, rows(g)) for h in range(3)]
        for step in range(steps):
            for z in range(PAIR):
                at = pl.ds(z * steps + step, 1)
                source[step, z, rows(g)] = (
                    waves[0, at] * coils[0] + waves[1, at] * coils[1] + waves[2, at] * coils[2]
                )

    @pl.loop(0, (nnz - 1) * CHUNKS)
    def _(c):
        s, q = 1 + c // CHUNKS, lax.rem(c, CHUNKS)
        load(s, q).wait()
        reaches = crosses[s - 1] == 1.0

        @pl.loop(0, span, unroll=UNROLL)
        def _(j):
            a = q * span + j
            for b in range(groups):
                packed = None
                for k in range(QUARTERS):
                    block = mine(raw, s, k, a, rows(b))
                    stiff[s, k * quarter + a, rows(b)] = block
                    moved = block if k == 0 else pltpu.roll(block, 2 * NIF * k, 1)
                    packed = moved if k == 0 else jnp.where(quarter_of == k, moved, packed)
                edge_stiff[s - 1, a, b] = jnp.where(reaches, packed, 0.0)

    @pl.loop(0, CHUNKS)
    def _(q):
        load(0, q).wait()

        @pl.loop(0, span, unroll=UNROLL)
        def _(j):
            a = q * span + j
            for k in range(QUARTERS):
                for b in range(groups):
                    stiff[0, k * quarter + a, rows(b)] = mine(raw, 0, k, a, rows(b))

    for g in range(groups):
        diag = jnp.zeros((ROWS, LANES), jnp.float32)
        for r in range(ROWS):
            diag = jnp.where(row == r, stiff[0, g * ROWS + r, rows(g)], diag)
        damp[rows(g)] = 1.0 / (1.0 + tau_step * (diag + play_gain))

    small[3].wait()
    small[4].wait()
    for copy in inputs:
        copy.wait()
    for z in range(PAIR):
        for g in range(groups):
            here = (z, rows(g))
            a = mine(start_in, *here)
            p = mine(level_in, *here).astype(jnp.float32) * play_quantum
            guess[here] = a
            field[here] = a
            begin[(0, *here)] = a
            state[here] = p
            begin[(1, *here)] = p

    def near_copy(slot):
        return pltpu.make_async_remote_copy(
            src_ref=near_out, dst_ref=near_in.at[slot],
            send_sem=near_send, recv_sem=near_recv.at[slot],
            device_id={"tm": other}, device_id_type=MESH,
        )

    def edge_copy(side, slot, z):
        return pltpu.make_async_remote_copy(
            src_ref=edge_out.at[z], dst_ref=edge_in.at[1 - side, slot, z],
            send_sem=edge_send.at[side, z], recv_sem=edge_recv.at[1 - side, slot, z],
            device_id={"space": part + 2 * side - 1}, device_id_type=MESH,
        )

    def pack(values):
        packs = []
        for j in range(lots):
            packed = values[j]
            for k in range(1, QUARTERS):
                moved = pltpu.roll(values[k * lots + j], 2 * NIF * k, 1)
                packed = jnp.where(quarter_of == k, moved, packed)
            packs.append(packed)
        return packs

    def send_edges(slot, z, more):
        @pl.when(has_left & more)
        def _():
            edge_copy(0, slot, z).start()

        @pl.when(has_right & more)
        def _():
            edge_copy(1, slot, z).start()

    def products(slots, g):
        sums = [[None] * ROWS for _ in range(PAIR)]
        for s in slots:
            for b in range(groups):
                vectors = [
                    guess[z, rows(b)] if s == 0 else picked[z, s - 1, rows(b)]
                    for z in range(PAIR)
                ]
                for r in range(ROWS):
                    block = stiff[s, g * ROWS + r, rows(b)]
                    for z in range(PAIR):
                        term = block * vectors[z]
                        sums[z][r] = term if sums[z][r] is None else sums[z][r] + term
        return [merge_rows(sums[z]) for z in range(PAIR)]

    def active(step, counter, z):
        count = jnp.broadcast_to(counts_all[z, pl.ds(step, 1)], (ROWS, LANES))
        return jnp.full((ROWS, LANES), counter, jnp.int32).astype(jnp.float32) < count

    def sweep(before, step, counter):
        done = step * NEWT + counter
        slot = lax.rem(before + done, 2)
        more = done < sweeps - 1

        @pl.loop(0, groups, unroll=8)
        def _(g):
            sums = products((0,), g)
            for z in range(PAIR):
                first[z, rows(g)] = sums[z]
            for s in range(1, nnz):
                for z in range(PAIR):
                    here = take(guess[z, rows(g)], index[s - 1])
                    picked[z, s - 1, rows(g)] = jnp.where(owner[s - 1] == 0, here, 0.0)

        near_copy(slot).wait()
        for s in range(1, nnz):
            where, whose = index[s - 1], owner[s - 1]
            for z in range(PAIR):
                for b in range(groups):
                    near = take(near_in[slot, z, rows(b)], where)
                    here = (z, s - 1, rows(b))
                    picked[here] = jnp.where(whose == 1, near, picked[here])

        @pl.loop(0, groups, unroll=8)
        def _(g):
            sums = products(range(1, nnz), g)
            for z in range(PAIR):
                first[z, rows(g)] += sums[z]

        for z in range(PAIR):
            works = active(step, counter, z)
            for g in range(groups):
                here = (z, rows(g))
                x = guess[here]
                bound = play(state[here], x, width_ref[rows(g)])
                resid = x - field[here] - tau_step * (
                    source[(step, *here)] - first[here] - play_gain * bound
                )
                x = jnp.where(works, x - resid * damp[rows(g)], x)
                guess[here] = x
                near_out[here] = x

        @pl.when(more)
        def _():
            near_copy(1 - slot).start()

        @pl.when(outer)
        def _():
            def restore(z):
                for j in range(lots):
                    packed = edge_out[z, j]
                    for k in range(QUARTERS):
                        here = (z, rows(k * lots + j))
                        back = packed if k == 0 else pltpu.roll(packed, LANES - 2 * NIF * k, 1)
                        guess[here] = jnp.where(at_edge, back, guess[here])

            for z in range(PAIR):
                @pl.when(has_left)
                def _():
                    edge_copy(0, slot, z).wait_send()
                    edge_copy(1, slot, z).wait_recv()

                @pl.when(has_right)
                def _():
                    edge_copy(1, slot, z).wait_send()
                    edge_copy(0, slot, z).wait_recv()

                came = [
                    jnp.where(even, edge_in[1, slot, z, j], edge_in[0, slot, z, j])
                    for j in range(lots)
                ]
                sums = [None] * quarter
                for s in range(nnz - 1):
                    for k in range(QUARTERS):
                        vectors = [take(came[j], edge_index[s, k]) for j in range(lots)]
                        for j in range(lots):
                            for a in range(quarter):
                                term = edge_stiff[s, a, k * lots + j] * vectors[j]
                                sums[a] = term if sums[a] is None else sums[a] + term
                partial = pack([guess[z, rows(g)] for g in range(groups)])
                works = jnp.where(active(step, counter, z), -tau_step, 0.0)
                if z > 0:
                    restore(z - 1)
                for j in range(lots):
                    total = merge_rows(sums[j * ROWS : (j + 1) * ROWS])
                    edge_out[z, j] = partial[j] + works * edge_damp[j] * total

                send_edges(1 - slot, z, more)

            restore(PAIR - 1)

    own = [pl.ds(g * ROWS, ROWS) for g in range(groups)]
    for j, packed in enumerate(pack([damp[g] for g in own])):
        edge_damp[j] = packed
    def open_round(before):
        near_out[...] = guess[...]
        near_copy(before % 2).start()

        @pl.when(outer)
        def _():
            for z in range(PAIR):
                for j, packed in enumerate(pack([guess[z, g] for g in own])):
                    edge_out[z, j] = packed
                send_edges(before % 2, z, True)

    open_round(0)
    for round_ in range(ITERS):
        before = round_ * sweeps

        @pl.loop(0, steps)
        def _(step):
            @pl.loop(0, NEWT)
            def _(counter):
                sweep(before, step, counter)

            for z in range(PAIR):
                for g in own:
                    x = guess[z, g]
                    state[z, g] = play(state[z, g], x, width_ref[g])
                    field[z, g] = x

        final = pair == pairs - 1
        ends = jnp.full((ROWS, LANES), pair, jnp.int32) == pairs - 1

        def scan_copy(kind, to, slot):
            return pltpu.make_async_remote_copy(
                src_ref=scan_out.at[round_, kind], dst_ref=scan_in.at[round_, slot, kind],
                send_sem=scan_send.at[round_, kind, to], recv_sem=scan_recv.at[round_, kind, slot],
                device_id={"tm": to * PAIR + core}, device_id_type=MESH,
            )

        for kind, fine in enumerate((guess, state)):
            for g in own:
                d = damp[g] if kind == 0 else 1.0
                extra = [fine[z, g] - d * begin[kind, z, g] for z in range(PAIR)]
                scan_out[round_, kind, g] = jnp.where(ends, fine[1, g], d * extra[0] + extra[1])
                begin[kind, 1, g] = extra[0]
            for to in range(pairs):
                @pl.when((pair != to) & (final | (pair < to)))
                def _():
                    scan_copy(kind, to, pair).start()

        for kind in range(2):
            for from_ in range(pairs):
                @pl.when((pair != from_) & ((from_ < pair) | (from_ == pairs - 1)))
                def _():
                    scan_copy(kind, from_, from_).wait_recv()

            @pl.when(final)
            def _():
                for g in own:
                    begin[kind, 0, g] = scan_out[round_, kind, g]

            @pl.when(pair < pairs - 1)
            def _():
                for g in own:
                    begin[kind, 0, g] = scan_in[round_, pairs - 1, kind, g]

            for from_ in range(pairs - 1):
                @pl.when(from_ < pair)
                def _():
                    for g in own:
                        d = damp[g] if kind == 0 else 1.0
                        begin[kind, 0, g] = (
                            d * d * begin[kind, 0, g] + scan_in[round_, from_, kind, g]
                        )
            for g in own:
                d = damp[g] if kind == 0 else 1.0
                begin[kind, 1, g] = d * begin[kind, 0, g] + begin[kind, 1, g]
                if round_ < ITERS - 1:
                    for z in range(PAIR):
                        if kind == 0:
                            guess[z, g] = begin[0, z, g]
                            field[z, g] = begin[0, z, g]
                        else:
                            state[z, g] = begin[1, z, g]
            if kind == 0 and round_ < ITERS - 1:
                open_round((round_ + 1) * sweeps)

        for kind in range(2):
            for to in range(pairs):
                @pl.when((pair != to) & (final | (pair < to)))
                def _():
                    scan_copy(kind, to, pair).wait_send()

    for kind in range(2):
        for g in own:
            last_out[kind, g] = begin[kind, 1 - core, g]
    swap = pltpu.make_async_remote_copy(
        src_ref=last_out, dst_ref=last_in, send_sem=last_send, recv_sem=last_recv,
        device_id={"tm": other}, device_id_type=MESH,
    )
    swap.start()
    swap.wait()
    for kind in range(2):
        for g in own:
            kept, came = begin[kind, core, g], last_in[kind, g]
            out_ref[kind, 0, g, tiles[0]] = jnp.where(mine_low, kept, came)
            out_ref[kind, 0, g, tiles[1]] = jnp.where(mine_low, came, kept)


def on_device(start_field, play_level, stiffness, columns, play_width, coil, newton_counts):
    slices, parts = lax.axis_size("tm"), lax.axis_size("space")
    nnz, blk, _, local = stiffness.shape
    pairs = slices // PAIR
    groups, steps = blk // ROWS, newton_counts.shape[1]
    quarter = blk // QUARTERS
    lots = quarter // ROWS
    stiffness = stiffness.reshape(nnz, QUARTERS, quarter, blk, local)
    wave_rows = -(-PAIR * steps // ROWS) * ROWS
    vmem = pl.BlockSpec(memory_space=pltpu.VMEM)
    whole, half = (blk, local), (blk, LANES)
    f32, i32 = jnp.float32, jnp.int32
    dma = pltpu.SemaphoreType.DMA
    both = pl.pallas_call(
        functools.partial(kernel, slices, parts),
        out_shape=jax.ShapeDtypeStruct((2, 1, *whole), f32),
        in_specs=[pl.BlockSpec(memory_space=pltpu.HBM)] * 7,
        out_specs=vmem,
        scratch_shapes=[
            pltpu.SMEM(newton_counts.shape, i32),
            pltpu.VMEM((PAIR, *whole), f32),
            pltpu.VMEM((PAIR, *whole), i32),
            pltpu.VMEM(columns.shape, i32),
            pltpu.VMEM(whole, f32),
            pltpu.VMEM(coil.shape, f32),
            pltpu.VMEM((ROWS, LANES), f32),
            pltpu.VMEM((PAIR, ROWS, LANES), f32),
            dma((6,)),
            pltpu.VMEM(stiffness.shape, f32),
            pltpu.VMEM((nnz, blk, *half), f32),
            pltpu.VMEM((nnz - 1, quarter, groups, ROWS, LANES), f32),
            pltpu.VMEM((PAIR, *half), f32),
            pltpu.VMEM((PAIR, *half), f32),
            pltpu.VMEM((PAIR, *half), f32),
            pltpu.VMEM((2, PAIR, *half), f32),
            pltpu.VMEM(half, f32),
            pltpu.VMEM(half, f32),
            pltpu.VMEM((PAIR, *half), f32),
            pltpu.VMEM((PAIR, nnz - 1, *half), f32),
            pltpu.VMEM((steps, PAIR, *half), f32),
            pltpu.VMEM((3, wave_rows, LANES), f32),
            pltpu.VMEM((nnz - 1, ROWS, LANES), i32),
            pltpu.VMEM((nnz - 1, ROWS, LANES), i32),
            pltpu.VMEM((nnz - 1, QUARTERS, ROWS, LANES), i32),
            pltpu.VMEM((nnz - 1, ROWS, LANES), f32),
            pltpu.VMEM((PAIR, *half), f32),
            pltpu.VMEM((2, PAIR, *half), f32),
            pltpu.VMEM((PAIR, lots, ROWS, LANES), f32),
            pltpu.VMEM((2, 2, PAIR, lots, ROWS, LANES), f32),
            pltpu.VMEM((lots, ROWS, LANES), f32),
            pltpu.VMEM((ITERS, 2, *half), f32),
            pltpu.VMEM((ITERS, pairs, 2, *half), f32),
            pltpu.VMEM((2, *half), f32),
            pltpu.VMEM((2, *half), f32),
            dma((nnz, CHUNKS)),
            dma((3,)),
            dma((3,)),
            dma(()),
            dma((2,)),
            dma((2, PAIR)),
            dma((2, 2, PAIR)),
            dma((ITERS, 2, pairs)),
            dma((ITERS, 2, pairs)),
            dma(()),
            dma(()),
        ],
        compiler_params=pltpu.CompilerParams(
            collective_id=0, has_side_effects=True, vmem_limit_bytes=40 * 1024 * 1024
        ),
        name="parareal",
    )(*[
        pltpu.with_memory_space_constraint(array, pltpu.HBM)
        for array in (
            start_field, play_level, stiffness, columns, play_width, coil, newton_counts
        )
    ])
    return both[0], both[1]


def solution(mesh):
    return jax.shard_map(
        on_device,
        mesh=mesh,
        in_specs=(
            P("tm", None, "space"),
            P("tm", None, "space"),
            P(None, None, None, "space"),
            P(None, "space"),
            P(None, "space"),
            P(None, None, "space"),
            P("tm", None),
        ),
        out_specs=(P("tm", None, "space"), P("tm", None, "space")),
        check_vma=False,
    )
```
